32 devices in a mesh: dp: 8 (over y, x, core), tensor: 4 (over z).
Axes of the slice: x: 2, y: 2, z: 4, core: 2. Of those that a mesh axis runs over, the one named last changes fastest.
Arguments:
- inputs: float32 [4096, 768], P(('dp', 'tensor')), may hold values from -6 to 6
- qkv_weight: bfloat16 [1, 768, 3, 768], P(None, 'dp', None, 'tensor'), as said below
- out_weight: bfloat16 [1, 768, 768], P(None, 'tensor', 'dp'), may hold values from -1.75 to 1.75
- fc_weight: bfloat16 [1, 768, 3072], P(None, 'dp', 'tensor'), may hold values from -0.21875 to 0.21875
- proj_weight: bfloat16 [1, 3072, 768], P(None, 'tensor', 'dp'), may hold values from -0.109375 to 0.109375
- vectors: float32 [1, 12, 768], P(None, None, ('dp', 'tensor')), as said below
- out_grad: float32 [4096, 768], P(('dp', 'tensor')), may hold values from -6 to 6
Outputs:
- outputs: float32 [4096, 768], P(('dp', 'tensor'))
- input_grad: float32 [4096, 768], P(('dp', 'tensor'))
- qkv_grad: float32 [1, 768, 3, 768], P(None, 'dp', None, 'tensor')
- out_weight_grad: float32 [1, 768, 768], P(None, 'tensor', 'dp')
- fc_grad: float32 [1, 768, 3072], P(None, 'dp', 'tensor')
- proj_grad: float32 [1, 3072, 768], P(None, 'tensor', 'dp')
- vector_grad: float32 [1, 12, 768], P(None, None, ('dp', 'tensor'))
The draws below stay inside these ranges and needn't reach their ends.
Inputs may be any that keep to these rules, and one draw needn't show every extreme that they name: `vectors`: gains lie near one, biases are of order 0.3. `qkv_weight`: entries are of order D ** -0.5.
All inputs are finite; a program needn't handle non-finite values.
Results may differ from the reference program's by a relative error of at most 0.018.
Values may be sent and summed in bfloat16 or wider, within the bound.
No kernel may reach another device: no remote copies, remote signals or barrier semaphores. Data moves between devices by JAX's collectives and lax.ppermute only.
A program may use at most 64 MiB of HBM per device.

```python
import math
import jax
import jax.numpy as jnp
from jax import lax

D = 768
HEADS = 12
HEAD_DIM = 64
FF = 3072
LAYERS = 1
SEQ_LEN = 256
VEC_ROWS = 12
TOKENS = 4096


def draw_qkv_weight(key, part):
    keys = jax.random.split(key, 1)
    shape = (LAYERS, D, 3, D)
    base = jax.random.truncated_normal(keys[0], -4.0, 4.0, shape, jnp.float32)
    return (base * D ** (-0.5)).astype(jnp.bfloat16)


def draw_vectors(key, part):
    keys = jax.random.split(key, 2)
    shape = (LAYERS, VEC_ROWS, D)
    noise = jax.random.normal(keys[1], shape, jnp.float32)
    rows = jnp.arange(VEC_ROWS)[None, :, None]
    is_gain = (rows == 0) | (rows == 5)
    gains = 1.0 + 0.3 * jnp.clip(noise, -1.5, 1.5)
    biases = 0.3 * jnp.clip(noise, -3.0, 3.0)
    return jnp.where(is_gain, gains, biases)


def spiked(drawn, own_key, source, target, blocks, factor):
    owner, partner = [(jnp.arange(drawn.shape[dim]) // (drawn.shape[dim] // blocks)).reshape([-1 if axis == dim else 1 for axis in range(drawn.ndim)]) for dim in (source, target)]
    chosen = jax.random.permutation(own_key, blocks)[partner]
    strong = (owner == chosen) | (owner == (partner + blocks // 2) % blocks)
    return jnp.where(strong, factor * drawn, drawn)


def level_of(own_key, dims, cuts, smallest, top_value):
    level, own = 1.0, jax.random.fold_in(own_key, 6)
    for position, parts in cuts:
        draws = jnp.exp(jax.random.uniform(jax.random.fold_in(own, position), (parts,), jnp.float32, smallest / len(cuts), top_value / len(cuts)))
        level = level * jnp.repeat(draws, dims[position] // parts).reshape([-1 if axis == position else 1 for axis in range(len(dims))])
    return level


def normal_values(key, dims, scale, bound, pieces=(), kind=jnp.bfloat16):
    values = jax.random.normal(key, dims, jnp.float32) * scale
    if len(pieces) > 0:
        values = level_of(key, dims, pieces, -0.22, 0.18) * values
    return jnp.clip(values, min=-bound, max=bound).astype(kind)


def bell_draw_with(own_key, shape, scale, limit, cuts, heavy, kind=jnp.bfloat16):
    array = scale * jax.random.normal(own_key, shape, jnp.float32)
    if cuts:
        array = array * level_of(own_key, shape, cuts, -0.22, 0.18)
    return jnp.clip(spiked(array, jax.random.fold_in(own_key, 3), *heavy), -limit, limit).astype(kind)


def setup_inputs(seed: int = 0) -> dict:
    key_list = jax.random.split(jax.random.key(seed), 8)
    inputs = normal_values(key_list[0], (TOKENS, D), 1.0, 6.0, ((0, 32),), jnp.float32)
    qkv_weight = draw_qkv_weight(jax.random.fold_in(key_list[7], 71), 0)
    out_weight = normal_values(key_list[2], (LAYERS, D, D), (max(D // 64, 4)) ** -0.5, 1.75, ((1, 4), (2, 8)))
    fc_weight = normal_values(key_list[3], (LAYERS, D, FF), D ** -0.5, 0.21875, ((1, 8), (2, 4)))
    proj_weight = normal_values(key_list[4], (LAYERS, FF, D), FF ** -0.5, 0.109375, ((1, 4), (2, 8)))
    vectors = draw_vectors(jax.random.fold_in(key_list[7], 71), 0)
    out_grad = bell_draw_with(key_list[6], (TOKENS, D), 1.0, 6.0, ((0, 32),), (0, 1, 32, 2.75), jnp.float32)
    return dict(inputs=inputs, qkv_weight=qkv_weight, out_weight=out_weight, fc_weight=fc_weight, proj_weight=proj_weight, vectors=vectors, out_grad=out_grad)


NORM_EPS = 1e-05
GELU_COEF = 0.7978845608028654
MASK_LOW = -1000000000.0

def layer_norm(rows, gain, shift):
    mean = lax.optimization_barrier(jnp.mean(rows, axis=-1, keepdims=True))
    centred = rows - mean
    variance = lax.optimization_barrier(jnp.mean(centred * centred, axis=-1, keepdims=True))
    inv_std = lax.rsqrt(variance + NORM_EPS)
    normed = centred * inv_std
    return (normed * gain + shift, normed, inv_std)

def layer_norm_back(grad_out, normed, inv_std, gain):
    grad_normed = grad_out * gain
    mean_one = lax.optimization_barrier(jnp.mean(grad_normed, axis=-1, keepdims=True))
    mean_two = lax.optimization_barrier(jnp.mean(grad_normed * normed, axis=-1, keepdims=True))
    grad_rows = inv_std * (grad_normed - mean_one - normed * mean_two)
    return (grad_rows, lax.optimization_barrier(jnp.sum(grad_out * normed, 0)), lax.optimization_barrier(jnp.sum(grad_out, 0)))

def gelu_parts(pre):
    inner = GELU_COEF * (pre + 0.044715 * pre * pre * pre)
    tanh_val = jnp.tanh(inner)
    value = 0.5 * pre * (1.0 + tanh_val)
    slope = 0.5 * (1.0 + tanh_val) + 0.5 * pre * (1.0 - tanh_val * tanh_val) * GELU_COEF * (1.0 + 3.0 * 0.044715 * pre * pre)
    return (value, slope)

def causal_mask(length):
    rows = lax.broadcasted_iota(jnp.int32, (length, length), 0)
    cols = lax.broadcasted_iota(jnp.int32, (length, length), 1)
    return rows >= cols

def attend(query, keys, values):
    scale = HEAD_DIM ** (-0.5)
    scores = jnp.einsum('qhd,khd->hqk', query.astype(jnp.float32), keys.astype(jnp.float32)) * scale
    scores = jnp.where(causal_mask(query.shape[0])[None], scores, MASK_LOW)
    top = lax.optimization_barrier(jnp.max(scores, axis=-1, keepdims=True))
    total = lax.optimization_barrier(jnp.sum(jnp.exp(scores - top), axis=-1, keepdims=True))
    log_total = top + jnp.log(total)
    probs = jnp.exp(scores - log_total).astype(jnp.bfloat16)
    context = jnp.einsum('hqk,khd->qhd', probs.astype(jnp.float32), values.astype(jnp.float32)).astype(jnp.bfloat16)
    return (context, log_total)

def attend_back(query, keys, values, log_total, grad_ctx):
    scale = HEAD_DIM ** (-0.5)
    scores = jnp.einsum('qhd,khd->hqk', query.astype(jnp.float32), keys.astype(jnp.float32)) * scale
    scores = jnp.where(causal_mask(query.shape[0])[None], scores, MASK_LOW)
    probs = jnp.exp(scores - log_total)
    probs_low = probs.astype(jnp.bfloat16)
    grad_ctx32 = grad_ctx.astype(jnp.float32)
    grad_values = jnp.einsum('hqk,qhd->khd', probs_low.astype(jnp.float32), grad_ctx32)
    grad_probs = jnp.einsum('qhd,khd->hqk', grad_ctx32, values.astype(jnp.float32))
    row_sum = lax.optimization_barrier(jnp.sum(probs * grad_probs, axis=-1, keepdims=True))
    grad_scores = (probs * (grad_probs - row_sum) * scale).astype(jnp.bfloat16).astype(jnp.float32)
    grad_query = jnp.einsum('hqk,khd->qhd', grad_scores, keys.astype(jnp.float32))
    grad_keys = jnp.einsum('hqk,qhd->khd', grad_scores, query.astype(jnp.float32))
    return (grad_query, grad_keys, grad_values)

def block_pass(x_rows, grad_rows, qkv_weight, out_weight, fc_weight, proj_weight, vectors):
    count = x_rows.shape[0]
    seq_count = count // SEQ_LEN
    saved = []
    resid = x_rows
    for layer in range(LAYERS):
        vec = vectors[layer]
        w_qkv = qkv_weight[layer].reshape(D, 3 * D)
        w_out = out_weight[layer]
        w_fc = fc_weight[layer]
        w_proj = proj_weight[layer]
        normed_out, normed1, inv1 = layer_norm(resid, vec[0], vec[1])
        a_rows = normed_out.astype(jnp.bfloat16)
        qkv = jnp.dot(a_rows, w_qkv, preferred_element_type=jnp.float32).reshape(count, 3, D)
        query = (qkv[:, 0] + vec[2]).astype(jnp.bfloat16).reshape(seq_count, SEQ_LEN, HEADS, HEAD_DIM)
        keys = qkv[:, 1].astype(jnp.bfloat16).reshape(seq_count, SEQ_LEN, HEADS, HEAD_DIM)
        values = (qkv[:, 2] + vec[3]).astype(jnp.bfloat16).reshape(seq_count, SEQ_LEN, HEADS, HEAD_DIM)
        context, log_total = jax.vmap(attend)(query, keys, values)
        ctx_flat = context.reshape(count, D)
        resid1 = resid + jnp.dot(ctx_flat, w_out, preferred_element_type=jnp.float32) + vec[4]
        normed_out2, normed2, inv2 = layer_norm(resid1, vec[5], vec[6])
        m_rows = normed_out2.astype(jnp.bfloat16)
        bias_fc = vec[8:].reshape(FF)
        pre = jnp.dot(m_rows, w_fc, preferred_element_type=jnp.float32) + bias_fc
        act, slope = gelu_parts(pre)
        act_low = act.astype(jnp.bfloat16)
        resid = resid1 + jnp.dot(act_low, w_proj, preferred_element_type=jnp.float32) + vec[7]
        saved.append((a_rows, normed1, inv1, query, keys, values, log_total, ctx_flat, normed2, inv2, m_rows, slope, act_low))
    outputs = resid
    grad = grad_rows
    grads = [None] * LAYERS
    for layer in reversed(range(LAYERS)):
        vec = vectors[layer]
        w_qkv = qkv_weight[layer].reshape(D, 3 * D)
        w_out = out_weight[layer]
        w_fc = fc_weight[layer]
        w_proj = proj_weight[layer]
        a_rows, normed1, inv1, query, keys, values, log_total, ctx_flat, normed2, inv2, m_rows, slope, act_low = saved[layer]
        g_bias_proj = lax.optimization_barrier(jnp.sum(grad, 0))
        grad_low = grad.astype(jnp.bfloat16)
        g_proj = jnp.dot(act_low.T, grad_low, preferred_element_type=jnp.float32)
        d_pre = jnp.dot(grad_low, w_proj.T, preferred_element_type=jnp.float32) * slope
        g_bias_fc = lax.optimization_barrier(jnp.sum(d_pre, 0))
        d_pre_low = d_pre.astype(jnp.bfloat16)
        g_fc = jnp.dot(m_rows.T, d_pre_low, preferred_element_type=jnp.float32)
        d_m = jnp.dot(d_pre_low, w_fc.T, preferred_element_type=jnp.float32)
        d_in, g_gain2, g_shift2 = layer_norm_back(d_m, normed2, inv2, vec[5])
        grad1 = grad + d_in
        g_bias_out = lax.optimization_barrier(jnp.sum(grad1, 0))
        grad1_low = grad1.astype(jnp.bfloat16)
        g_out = jnp.dot(ctx_flat.T, grad1_low, preferred_element_type=jnp.float32)
        d_ctx = jnp.dot(grad1_low, w_out.T, preferred_element_type=jnp.float32).astype(jnp.bfloat16)
        d_ctx = d_ctx.reshape(count // SEQ_LEN, SEQ_LEN, HEADS, HEAD_DIM)
        d_query, d_keys, d_values = jax.vmap(attend_back)(query, keys, values, log_total, d_ctx)
        d_query = d_query.reshape(count, D)
        d_keys = d_keys.reshape(count, D)
        d_values = d_values.reshape(count, D)
        g_bias_q = lax.optimization_barrier(jnp.sum(d_query, 0))
        g_bias_v = lax.optimization_barrier(jnp.sum(d_values, 0))
        d_qkv = jnp.stack([d_query, d_keys, d_values], axis=1).astype(jnp.bfloat16).reshape(count, 3 * D)
        g_qkv = jnp.dot(a_rows.T, d_qkv, preferred_element_type=jnp.float32).reshape(D, 3, D)
        d_a = jnp.dot(d_qkv, w_qkv.T, preferred_element_type=jnp.float32)
        d_in1, g_gain1, g_shift1 = layer_norm_back(d_a, normed1, inv1, vec[0])
        grad = grad1 + d_in1
        head_rows = jnp.stack([g_gain1, g_shift1, g_bias_q, g_bias_v, g_bias_out, g_gain2, g_shift2, g_bias_proj])
        vec_grad = jnp.concatenate([head_rows, g_bias_fc.reshape(FF // D, D)], axis=0)
        grads[layer] = (g_qkv, g_out, g_fc, g_proj, vec_grad)
    stacked = tuple((jnp.stack([grads[i][j] for i in range(LAYERS)]) for j in range(5)))
    return (outputs, grad, stacked)

def reference(inputs, qkv_weight, out_weight, fc_weight, proj_weight, vectors, out_grad):
    seq_total = TOKENS // SEQ_LEN
    group = math.gcd(seq_total, 8)
    blocks = seq_total // group
    x_blocks = inputs.reshape(blocks, group * SEQ_LEN, D)
    g_blocks = out_grad.reshape(blocks, group * SEQ_LEN, D)
    init = (jnp.zeros((LAYERS, D, 3, D), jnp.float32), jnp.zeros((LAYERS, D, D), jnp.float32), jnp.zeros((LAYERS, D, FF), jnp.float32), jnp.zeros((LAYERS, FF, D), jnp.float32), jnp.zeros((LAYERS, VEC_ROWS, D), jnp.float32))

    def step(carry, pair):
        outs, grad_in, grads = block_pass(pair[0], pair[1], qkv_weight, out_weight, fc_weight, proj_weight, vectors)
        return (tuple((c + g for c, g in zip(carry, grads))), (outs, grad_in))
    totals, (outs, grad_ins) = lax.scan(step, init, (x_blocks, g_blocks))
    return (outs.reshape(TOKENS, D), grad_ins.reshape(TOKENS, D), totals[0], totals[1], totals[2], totals[3], totals[4])
```

```python
import jax
import jax.numpy as jnp
from jax import lax
from jax.experimental import pallas as pl
from jax.experimental.pallas import tpu as pltpu
from jax.sharding import PartitionSpec as P

HEAD_DIM = 64
NORM_EPS = 1e-05
GELU_COEF = 0.7978845608028654
MASK_LOW = -1000000000.0
SCALE = HEAD_DIM ** (-0.5)
BF16 = jnp.bfloat16
F32 = jnp.float32
NN = ((1,), (0,))
NT = ((1,), (1,))
TN = ((0,), (0,))


def dot(a, b, dims=NN):
    return lax.dot_general(a, b, (dims, ((), ())), preferred_element_type=F32)


def swap(value, axis, bits):
    size = lax.axis_size(axis)
    return lax.ppermute(value, axis, [(i, i ^ bits) for i in range(size)])


def normalize(rows):
    mean = jnp.mean(rows, axis=-1, keepdims=True)
    centred = rows - mean
    variance = jnp.mean(centred * centred, axis=-1, keepdims=True)
    inv_std = lax.rsqrt(variance + NORM_EPS)
    return (centred * inv_std, inv_std)


def norm_back(grad_out, normed, inv_std, gain):
    grad_normed = grad_out * gain
    mean_one = jnp.mean(grad_normed, axis=-1, keepdims=True)
    mean_two = jnp.mean(grad_normed * normed, axis=-1, keepdims=True)
    return inv_std * (grad_normed - mean_one - normed * mean_two)


def gelu_parts(pre):
    square = pre * pre
    inner = GELU_COEF * (pre + 0.044715 * square * pre)
    tanh_val = jnp.tanh(inner)
    half = 0.5 * (1.0 + tanh_val)
    value = pre * half
    slope = half + 0.5 * pre * (1.0 - tanh_val * tanh_val) * GELU_COEF * (
        1.0 + 3.0 * 0.044715 * square
    )
    return (value, slope)


def column_sum(value):
    return jnp.sum(value, axis=0, keepdims=True)


def call(body, name, outs, args, scratch=(), spaces=None):
    spaces = spaces or {}
    in_specs = [
        pl.BlockSpec(memory_space=spaces.get(n, pltpu.VMEM)) for n in range(len(args))
    ]
    return pl.pallas_call(
        body,
        name=name,
        out_shape=[jax.ShapeDtypeStruct(shape, dtype) for shape, dtype in outs],
        in_specs=in_specs,
        out_specs=[pl.BlockSpec(memory_space=pltpu.VMEM) for _ in outs],
        scratch_shapes=list(scratch),
        compiler_params=pltpu.CompilerParams(vmem_limit_bytes=56 * 1024 * 1024),
    )(*args)


def bit_orders():
    count = lax.axis_size("dp").bit_length() - 1
    bits = [1 << b for b in range(1, count)]
    return (bits + [1], bits[::-1] + [1])


def gather_pieces(piece):
    shards_held = []
    for value, order in zip((piece[None], swap(piece[None], "tensor", 2)), bit_orders()):
        held = [((0,), value)]
        for bit in order:
            while len(held) > 4:
                held = [
                    (held[n][0] + held[n + 1][0], jnp.concatenate([held[n][1], held[n + 1][1]]))
                    for n in range(0, len(held), 2)
                ]
            held = held + [
                (tuple(k ^ bit for k in ks), swap(v, "dp", bit)) for ks, v in held
            ]
        shards_held.append(held)
    return shards_held


def assembled(held):
    ks = [k for group, _ in held for k in group]
    stacked = jnp.concatenate([v for _, v in held])
    slot = [ks.index(k) for k in range(len(ks))]
    stacked = jnp.stack([stacked[n] for n in slot])
    whole = jnp.take(stacked, lax.axis_index("dp") ^ jnp.arange(len(ks)), axis=0)
    return whole.reshape(1, -1, whole.shape[-1])


def piece_plan(pieces):
    aligned = pieces[0][0][1].shape[1] % 16 == 0
    arrays, plan = [], []
    for s, held in enumerate(pieces):
        if not aligned:
            plan.append((len(arrays), 0, s, None))
            arrays.append(assembled(held))
            continue
        for ks, value in held:
            plan += [(len(arrays), slot, s, k) for slot, k in enumerate(ks)]
            arrays.append(value)
    return arrays, plan


def place_pieces(refs, plan, dst_ref, sems, me):
    copies = []
    for n, (array, slot, s, k) in enumerate(plan):
        rows = refs[array].shape[1]
        if k is None:
            target = dst_ref.at[s]
        else:
            start = pl.multiple_of(jnp.bitwise_xor(me, k) * rows, 16)
            target = dst_ref.at[s, pl.ds(start, rows), :]
        copies.append(pltpu.make_async_copy(refs[array].at[slot], target, sems.at[n]))
    for copy in copies:
        copy.start()
    return copies


def relative_evens(shard):
    count = lax.axis_size("dp")
    bits = count.bit_length() - 1
    evens = list(range(0, count, 2))
    if shard == 1:
        evens.sort(key=lambda k: [k >> b & 1 for b in range(1, bits)])
    return evens


def put_grad(grad, s, scratch, keep_ref, send_ref, me, rows):
    if rows % 16:
        keep_ref[...] = grad
        return
    scratch[...] = grad
    for n, k in enumerate(relative_evens(s)):
        for k_of, ref in ((k, keep_ref), (k ^ 1, send_ref)):
            start = pl.multiple_of(jnp.bitwise_xor(me, k_of) * rows, 16)
            ref[n] = scratch[pl.ds(start, rows), :].astype(ref.dtype)


def grad_shapes(width, rows, cols):
    if rows % 16:
        return [((width, cols), F32), ((8, 128), BF16)] * 2
    half = width // rows // 2
    return [((half, rows, cols), F32), ((half, rows, cols), BF16)] * 2


def scatter_grad(parts, rows):
    sums = []
    me = lax.axis_index("dp")
    for s in range(2):
        keep, send = parts[2 * s : 2 * s + 2]
        if rows % 16:
            blocks = keep.reshape(-1, rows, keep.shape[-1])
            evens = jnp.array(relative_evens(s))
            keep = jnp.take(blocks, me ^ evens, axis=0)
            send = jnp.take(blocks, me ^ evens ^ 1, axis=0).astype(BF16)
        now = keep + swap(send, "dp", 1).astype(F32)
        for bit in bit_orders()[s][:-1][::-1]:
            half = now.shape[0] // 2
            sent = now[half:].astype(BF16)
            now = now[:half] + swap(sent, "dp", bit).astype(F32)
        sums.append(now[0])
    return sums[0] + swap(sums[1].astype(BF16), "tensor", 2).astype(F32)


def gather_vectors(value, index, count):
    rows, cols = value.shape
    spread = lax.dynamic_update_slice(jnp.zeros((rows, count * cols), F32), value, (0, index * cols))
    return sum_everywhere(spread)


def sum_everywhere(value):
    for bit in bit_orders()[0][::-1]:
        value = value + swap(value, "dp", bit)
    value = value + swap(value, "tensor", 2)
    return value + swap(value, "tensor", 1)


def norm_first_body(x_ref, g_ref, xh_ref, dy_ref, sum_ref):
    xh_ref[...] = normalize(x_ref[...])[0].astype(BF16)
    grad = g_ref[...]
    dy_ref[...] = grad.astype(BF16)
    sum_ref[...] = column_sum(grad)


def causal_mask(length):
    rows = lax.broadcasted_iota(jnp.int32, (length, length), 0)
    cols = lax.broadcasted_iota(jnp.int32, (length, length), 1)
    return rows >= cols


def attend_body(plan, n_arrays, head_cols, *refs):
    ids, own, other, vec, biases = refs[:5]
    pieces = refs[5 : 5 + n_arrays]
    w, qkv_out, ctx_out, lse_out, a_out, keep, send, total, sems = refs[5 + n_arrays :]
    me, role = ids[0], ids[1]
    copies = place_pieces(pieces, plan, w, sems, me)
    rows = own.shape[0]
    gain, shift = vec[0:1, :], vec[1:2, :]
    for ref, at in ((own, role), (other, 1 - role)):
        a_rows = ref[...].astype(F32) * gain + shift
        a_out[pl.ds(pl.multiple_of(at * rows, rows), rows), :] = a_rows.astype(BF16)
    for copy in copies:
        copy.wait()
    seq = 2 * rows
    a_rows = a_out[...]
    mask = causal_mask(seq)
    lane = lax.broadcasted_iota(jnp.int32, (seq, 128), 1)
    lse_all = jnp.zeros((seq, 128), F32)
    heads = head_cols // HEAD_DIM
    attn = None
    for s in range(2):
        qkv = dot(a_rows, w[s, :, : 3 * head_cols]) + biases[s : s + 1, :]
        qkv = qkv.astype(BF16)
        qkv_out[s] = qkv
        parts = []
        for h in range(heads):
            q, k, v = (
                qkv[:, n * head_cols + h * HEAD_DIM : n * head_cols + (h + 1) * HEAD_DIM]
                for n in range(3)
            )
            scores = jnp.where(mask, dot(q, k, NT) * SCALE, MASK_LOW)
            top = jnp.max(scores, axis=-1, keepdims=True)
            lse = top + jnp.log(jnp.sum(jnp.exp(scores - top), axis=-1, keepdims=True))
            lse_all = jnp.where(lane == s * heads + h, lse, lse_all)
            probs = jnp.exp(scores - lse).astype(BF16)
            parts.append(dot(probs, v).astype(BF16))
        ctx = jnp.concatenate(parts, axis=1)
        ctx_out[s] = ctx
        add = dot(ctx, w[s, :, 3 * head_cols :], NT)
        attn = add if attn is None else attn + add
    lse_out[...] = lse_all
    total[...] = attn
    keep[...] = total[pl.ds(pl.multiple_of(role * rows, rows), rows), :]
    send[...] = total[pl.ds(pl.multiple_of((1 - role) * rows, rows), rows), :].astype(BF16)


def norm_second_body(x_ref, keep_ref, recv_ref, vec_ref, resid_ref, m_ref):
    resid = x_ref[...] + (keep_ref[...] + recv_ref[...].astype(F32)) + vec_ref[4:5, :]
    resid_ref[...] = resid
    normed, _ = normalize(resid)
    m_ref[...] = (normed * vec_ref[5:6, :] + vec_ref[6:7, :]).astype(BF16)


def feed_body(plan, n_arrays, hidden, *refs):
    ids, m_own, m_other, dy_own, dy_other, bias = refs[:6]
    pieces = refs[6 : 6 + n_arrays]
    m_out, dy_out, act_out, dpre_out, dm_keep, dm_send, br_keep, br_send, sum_out, w, sems = refs[
        6 + n_arrays :
    ]
    copies = place_pieces(pieces, plan, w, sems, ids[0])
    rows = m_own.shape[0]
    m_out[:rows] = m_own[...]
    m_out[rows:] = m_other[...]
    dy_out[:rows] = dy_own[...]
    dy_out[rows:] = dy_other[...]
    m, dy = m_out[...], dy_out[...]
    for copy in copies:
        copy.wait()
    d_m = branch = None
    for s in range(2):
        w_fc, w_proj = w[s, :, :hidden], w[s, :, hidden:]
        pre = dot(m, w_fc) + bias[s : s + 1, :]
        act, slope = gelu_parts(pre)
        act_low = act.astype(BF16)
        act_out[s] = act_low
        d_pre = dot(dy, w_proj) * slope
        sum_out[s : s + 1, :] = column_sum(d_pre)
        d_pre_low = d_pre.astype(BF16)
        dpre_out[s] = d_pre_low
        one, two = dot(d_pre_low, w_fc, NT), dot(act_low, w_proj, NT)
        d_m = one if d_m is None else d_m + one
        branch = two if branch is None else branch + two
    dm_keep[...] = d_m[:rows]
    dm_send[...] = d_m[rows:].astype(BF16)
    br_keep[...] = branch[:rows]
    br_send[...] = branch[rows:].astype(BF16)


def feed_grad_body(block_rows, hidden, ids, m_ref, dy_ref, act_ref, dpre_ref, *refs):
    outs, scratch = refs[:4], refs[4]
    for s in range(2):
        grad = jnp.concatenate(
            [dot(m_ref[...], dpre_ref[s], TN), dot(dy_ref[...], act_ref[s], TN)], axis=1
        )
        put_grad(grad, s, scratch, outs[2 * s], outs[2 * s + 1], ids[0], block_rows)


def norm_second_back_body(resid_ref, keep_ref, recv_ref, grad_ref, vec_ref, grad1_ref, dz_ref, sum_ref):
    d_m = keep_ref[...] + recv_ref[...].astype(F32)
    normed, inv = normalize(resid_ref[...])
    grad1 = grad_ref[...] + norm_back(d_m, normed, inv, vec_ref[5:6, :])
    grad1_ref[...] = grad1
    dz_ref[...] = grad1.astype(BF16)
    sum_ref[0:1, :] = column_sum(grad1)
    sum_ref[1:2, :] = column_sum(d_m * normed)
    sum_ref[2:3, :] = column_sum(d_m)


def attend_back_body(head_cols, ids, own, other, xh_own, xh_other, w, qkv_ref, lse_ref, *refs):
    dz_out, dqkv_out, keep, send, sum_wide, sum_heads, total, normed = refs
    role = ids[1]
    rows = own.shape[0]
    seq = 2 * rows
    for ref, to, kind in ((own, dz_out, 0), (other, dz_out, 1), (xh_own, normed, 0), (xh_other, normed, 1)):
        at = role if kind == 0 else 1 - role
        to[pl.ds(pl.multiple_of(at * rows, rows), rows), :] = ref[...]
    dz = dz_out[...]
    mask = causal_mask(seq)
    heads = head_cols // HEAD_DIM
    d_a = None
    for s in range(2):
        d_ctx_all = dot(dz, w[s, :, 3 * head_cols :]).astype(BF16)
        d_parts = [[], [], []]
        qkv = qkv_ref[s]
        for h in range(heads):
            q, k, v = (
                qkv[:, n * head_cols + h * HEAD_DIM : n * head_cols + (h + 1) * HEAD_DIM]
                for n in range(3)
            )
            d_ctx = d_ctx_all[:, h * HEAD_DIM : (h + 1) * HEAD_DIM]
            head = s * heads + h
            scores = jnp.where(mask, dot(q, k, NT) * SCALE, MASK_LOW)
            probs = jnp.exp(scores - lse_ref[:, head : head + 1])
            d_parts[2].append(dot(probs.astype(BF16), d_ctx, TN))
            d_probs = dot(d_ctx, v, NT)
            row_sum = jnp.sum(probs * d_probs, axis=-1, keepdims=True)
            d_scores = (probs * (d_probs - row_sum) * SCALE).astype(BF16)
            d_parts[0].append(dot(d_scores, k))
            d_parts[1].append(dot(d_scores, q, TN))
        d_qkv = jnp.concatenate(d_parts[0] + d_parts[1] + d_parts[2], axis=1)
        sum_heads[s : s + 1, :] = column_sum(d_qkv)
        d_qkv = d_qkv.astype(BF16)
        dqkv_out[s] = d_qkv
        add = dot(d_qkv, w[s, :, : 3 * head_cols], NT)
        d_a = add if d_a is None else d_a + add
    total[...] = d_a
    sum_wide[0:1, :] = column_sum(d_a * normed[...].astype(F32))
    sum_wide[1:2, :] = column_sum(d_a)
    keep[...] = total[pl.ds(pl.multiple_of(role * rows, rows), rows), :]
    send[...] = total[pl.ds(pl.multiple_of((1 - role) * rows, rows), rows), :].astype(BF16)


def attend_grad_body(block_rows, head_cols, ids, a_ref, dz_ref, dqkv_ref, ctx_ref, *refs):
    wide, heads_sum, second, fc_sum, bp_sum = refs[:5]
    outs, vec_out, scratch = refs[5:9], refs[9], refs[10]
    z = ids[2]
    for s in range(2):
        grad = jnp.concatenate(
            [dot(a_ref[...], dqkv_ref[s], TN), dot(dz_ref[...], ctx_ref[s], TN)], axis=1
        )
        put_grad(grad, s, scratch, outs[2 * s], outs[2 * s + 1], ids[0], block_rows)
    vec_out[0:2, :] = wide[0:2, :]
    vec_out[4:7, :] = second[0:3, :]
    vec_out[7:8, :] = bp_sum[...]

    def placed(value, t):
        here = jnp.where(z == t, value[0:1, :], jnp.zeros_like(value[0:1, :]))
        return here + jnp.where(jnp.bitwise_xor(z, 2) == t, value[1:2, :], jnp.zeros_like(here))

    sums = heads_sum[...]
    n_z = vec_out.shape[1] // head_cols
    for row, part in ((2, 0), (3, 2)):
        value = sums[:, part * head_cols : (part + 1) * head_cols]
        vec_out[row : row + 1, :] = jnp.concatenate([placed(value, t) for t in range(n_z)], axis=1)
    for t in range(vec_out.shape[0] - 8):
        vec_out[8 + t : 9 + t, :] = placed(fc_sum[...], t)


def norm_first_back_body(x_ref, keep_ref, recv_ref, grad1_ref, vec_ref, out_ref):
    d_a = keep_ref[...] + recv_ref[...].astype(F32)
    normed, inv = normalize(x_ref[...])
    out_ref[...] = grad1_ref[...] + norm_back(d_a, normed, inv, vec_ref[0:1, :])


def shards(inputs, qkv_weight, out_weight, fc_weight, proj_weight, vectors, out_grad):
    rows, width = inputs.shape
    head_cols = qkv_weight.shape[3]
    hidden = fc_weight.shape[2]
    block_rows = qkv_weight.shape[1]
    vec_rows, vec_cols = vectors.shape[1:]
    n_z = lax.axis_size("tensor")
    n_dp = lax.axis_size("dp")
    z = lax.axis_index("tensor")
    me = lax.axis_index("dp")
    shard_ids = (z, z ^ 2)
    ids = jnp.stack([me, z & 1, z]).astype(jnp.int32)
    smem = {0: pltpu.SMEM}
    row = (rows, width)
    seq = 2 * rows
    both = (seq, width)

    part_a = jnp.concatenate(
        [qkv_weight[0].reshape(block_rows, 3 * head_cols), out_weight[0].T], axis=1
    )
    part_b = jnp.concatenate([fc_weight[0], proj_weight[0].T], axis=1)
    normed1, dy, bp_sum = call(
        norm_first_body, "norm_first", [(row, BF16), (row, BF16), ((1, width), F32)], (inputs, out_grad)
    )
    normed1_other = swap(normed1, "tensor", 1)
    arrays_a, plan_a = piece_plan(gather_pieces(part_a))
    vec = gather_vectors(vectors[0], me * n_z + z, n_dp * n_z)
    dy_other = swap(dy, "tensor", 1)
    arrays_b, plan_b = piece_plan(gather_pieces(part_b))

    def of_shard(table):
        return jnp.stack([lax.dynamic_index_in_dim(table, s, 0, False) for s in shard_ids])

    bias_q = of_shard(vec[2].reshape(n_z, head_cols))
    bias_v = of_shard(vec[3].reshape(n_z, head_cols))
    biases = jnp.concatenate([bias_q, jnp.zeros_like(bias_q), bias_v], axis=1)
    bias_fc = of_shard(vec[8:].reshape(n_z, hidden))

    def any_space(first, arrays):
        return {**smem, **{first + n: pl.ANY for n in range(len(arrays))}}

    w_a, qkv, ctx, lse, a_seq, attn_keep, attn_send = call(
        lambda *refs: attend_body(plan_a, len(arrays_a), head_cols, *refs),
        "attend",
        [
            ((2, width, 4 * head_cols), BF16),
            ((2, seq, 3 * head_cols), BF16),
            ((2, seq, head_cols), BF16),
            ((seq, 128), F32),
            (both, BF16),
            (row, F32),
            (row, BF16),
        ],
        (ids, normed1, normed1_other, vec, biases, *arrays_a),
        [pltpu.VMEM(both, F32), pltpu.SemaphoreType.DMA((len(plan_a),))],
        any_space(5, arrays_a),
    )
    resid1, m = call(
        norm_second_body,
        "norm_second",
        [(row, F32), (row, BF16)],
        (inputs, attn_keep, swap(attn_send, "tensor", 1), vec),
    )
    m_other = swap(m, "tensor", 1)
    m_both, dy_both, act, d_pre, dm_keep, dm_send, br_keep, br_send, fc_sum = call(
        lambda *refs: feed_body(plan_b, len(arrays_b), hidden, *refs),
        "feed",
        [
            (both, BF16),
            (both, BF16),
            ((2, seq, hidden), BF16),
            ((2, seq, hidden), BF16),
            (row, F32),
            (row, BF16),
            (row, F32),
            (row, BF16),
            ((2, hidden), F32),
        ],
        (ids, m, m_other, dy, dy_other, bias_fc, *arrays_b),
        [pltpu.VMEM((2, width, 2 * hidden), BF16), pltpu.SemaphoreType.DMA((len(plan_b),))],
        any_space(6, arrays_b),
    )
    dm_recv = swap(dm_send, "tensor", 1)
    parts_b = call(
        lambda *refs: feed_grad_body(block_rows, hidden, *refs),
        "feed_grad",
        grad_shapes(width, block_rows, 2 * hidden),
        (ids, m_both, dy_both, act, d_pre),
        [pltpu.VMEM((width, 2 * hidden), F32)],
        smem,
    )
    grad1, dz, second_sums = call(
        norm_second_back_body,
        "norm_second_back",
        [(row, F32), (row, BF16), ((3, width), F32)],
        (resid1, dm_keep, dm_recv, out_grad, vec),
    )
    dz_other = swap(dz, "tensor", 1)
    outputs = resid1 + (br_keep + swap(br_send, "tensor", 1).astype(F32)) + vec[7]
    b_grad = scatter_grad(parts_b, block_rows)
    dz_seq, d_qkv, da_keep, da_send, wide_sums, head_sums = call(
        lambda *refs: attend_back_body(head_cols, *refs),
        "attend_back",
        [
            (both, BF16),
            ((2, seq, 3 * head_cols), BF16),
            (row, F32),
            (row, BF16),
            ((2, width), F32),
            ((2, 3 * head_cols), F32),
        ],
        (ids, dz, dz_other, normed1, normed1_other, w_a, qkv, lse),
        [pltpu.VMEM(both, F32), pltpu.VMEM(both, BF16)],
        smem,
    )
    da_recv = swap(da_send, "tensor", 1)
    *parts_a, vec_sum = call(
        lambda *refs: attend_grad_body(block_rows, head_cols, *refs),
        "attend_grad",
        grad_shapes(width, block_rows, 4 * head_cols) + [((vec_rows, width), F32)],
        (ids, a_seq, dz_seq, d_qkv, ctx, wide_sums, head_sums, second_sums, fc_sum, bp_sum),
        [pltpu.VMEM((width, 4 * head_cols), F32)],
        smem,
    )
    a_grad = scatter_grad(parts_a, block_rows)
    vec_sum = sum_everywhere(vec_sum)
    vector_grad = lax.dynamic_slice_in_dim(vec_sum, (me * n_z + z) * vec_cols, vec_cols, 1)
    (input_grad,) = call(
        norm_first_back_body,
        "norm_first_back",
        [(row, F32)],
        (inputs, da_keep, da_recv, grad1, vec),
    )
    qkv_grad = a_grad[:, : 3 * head_cols].reshape(block_rows, 3, head_cols)
    return (
        outputs,
        input_grad,
        qkv_grad[None],
        a_grad[:, 3 * head_cols :].T[None],
        b_grad[None, :, :hidden],
        b_grad[:, hidden:].T[None],
        vector_grad[None],
    )


def solution(mesh):
    rows = P(("dp", "tensor"), None)
    weights = (
        P(None, "dp", None, "tensor"),
        P(None, "tensor", "dp"),
        P(None, "dp", "tensor"),
        P(None, "tensor", "dp"),
        P(None, None, ("dp", "tensor")),
    )
    return jax.shard_map(
        shards,
        mesh=mesh,
        in_specs=(rows, *weights, rows),
        out_specs=(rows, rows, *weights),
        check_vma=False,
    )
```

```python
import jax
import jax.numpy as jnp
from jax import lax
from jax.experimental import pallas as pl
from jax.experimental.pallas import tpu as pltpu
from jax.sharding import PartitionSpec as P

HEAD_DIM = 64
NORM_EPS = 1e-05
GELU_COEF = 0.7978845608028654
MASK_LOW = -1000000000.0
SCALE = HEAD_DIM ** (-0.5)
BF16 = jnp.bfloat16
F32 = jnp.float32
NN = ((1,), (0,))
NT = ((1,), (1,))
TN = ((0,), (0,))


def dot(a, b, dims=NN):
    return lax.dot_general(a, b, (dims, ((), ())), preferred_element_type=F32)


def swap(value, axis, bits):
    size = lax.axis_size(axis)
    return lax.ppermute(value, axis, [(i, i ^ bits) for i in range(size)])


def normalize(rows):
    mean = jnp.mean(rows, axis=-1, keepdims=True)
    centred = rows - mean
    variance = jnp.mean(centred * centred, axis=-1, keepdims=True)
    inv_std = lax.rsqrt(variance + NORM_EPS)
    return (centred * inv_std, inv_std)


def norm_back(grad_out, normed, inv_std, gain):
    grad_normed = grad_out * gain
    mean_one = jnp.mean(grad_normed, axis=-1, keepdims=True)
    mean_two = jnp.mean(grad_normed * normed, axis=-1, keepdims=True)
    return inv_std * (grad_normed - mean_one - normed * mean_two)


def gelu_parts(pre):
    square = pre * pre
    inner = GELU_COEF * (pre + 0.044715 * square * pre)
    tanh_val = jnp.tanh(inner)
    half = 0.5 * (1.0 + tanh_val)
    value = pre * half
    slope = half + 0.5 * pre * (1.0 - tanh_val * tanh_val) * GELU_COEF * (
        1.0 + 3.0 * 0.044715 * square
    )
    return (value, slope)


def column_sum(value):
    return jnp.sum(value, axis=0, keepdims=True)


def together(*values):
    return lax.optimization_barrier(values)


def call(body, name, micros, outs, args, scratch=(), spaces=None):
    spaces = spaces or {}
    in_specs = [
        pl.BlockSpec(memory_space=spaces.get(n, pltpu.VMEM)) for n in range(len(args))
    ]
    return pl.pallas_call(
        body,
        name=name,
        out_shape=[jax.ShapeDtypeStruct(shape, dtype) for shape, dtype in outs],
        in_specs=in_specs,
        out_specs=[pl.BlockSpec(memory_space=pltpu.VMEM) for _ in outs],
        scratch_shapes=list(scratch),
        compiler_params=pltpu.CompilerParams(vmem_limit_bytes=56 * 1024 * 1024),
        cost_estimate=pl.CostEstimate(
            flops=int(micros * 5e7), bytes_accessed=int(micros * 1e5), transcendentals=0
        ),
    )(*args)


def bit_orders():
    count = lax.axis_size("dp").bit_length() - 1
    bits = [1 << b for b in range(1, count)]
    return (bits + [1], bits[::-1] + [1])


def gather_start(piece):
    return [[((0,), piece[None])], [((0,), swap(piece[None], "tensor", 2))]]


def gather_stage(pieces, stage):
    out = []
    for held, order in zip(pieces, bit_orders()):
        bit = order[stage]
        while len(held) > 4:
            held = [
                (held[n][0] + held[n + 1][0], jnp.concatenate([held[n][1], held[n + 1][1]]))
                for n in range(0, len(held), 2)
            ]
        out.append(held + [(tuple(k ^ bit for k in ks), swap(v, "dp", bit)) for ks, v in held])
    return out


def tied(pieces, *values):
    flat, tree = jax.tree.flatten([[v for _, v in held] for held in pieces])
    done = together(*flat, *values)
    arrays = jax.tree.unflatten(tree, done[: len(flat)])
    pieces = [
        [(ks, v) for (ks, _), v in zip(held, new)] for held, new in zip(pieces, arrays)
    ]
    return (pieces, *done[len(flat) :])


def assembled(held):
    ks = [k for group, _ in held for k in group]
    stacked = jnp.concatenate([v for _, v in held])
    slot = [ks.index(k) for k in range(len(ks))]
    stacked = jnp.stack([stacked[n] for n in slot])
    whole = jnp.take(stacked, lax.axis_index("dp") ^ jnp.arange(len(ks)), axis=0)
    return whole.reshape(1, -1, whole.shape[-1])


def piece_plan(pieces):
    aligned = pieces[0][0][1].shape[1] % 16 == 0
    arrays, plan = [], []
    for s, held in enumerate(pieces):
        if not aligned:
            plan.append((len(arrays), 0, s, None))
            arrays.append(assembled(held))
            continue
        for ks, value in held:
            plan += [(len(arrays), slot, s, k) for slot, k in enumerate(ks)]
            arrays.append(value)
    return arrays, plan


def place_pieces(refs, plan, dst_refs, sems, me):
    copies = []
    for n, (array, slot, s, k) in enumerate(plan):
        rows = refs[array].shape[1]
        if k is None:
            target = dst_refs[s]
        else:
            start = pl.multiple_of(jnp.bitwise_xor(me, k) * rows, 16)
            target = dst_refs[s].at[pl.ds(start, rows), :]
        copies.append(pltpu.make_async_copy(refs[array].at[slot], target, sems.at[n]))
    for copy in copies:
        copy.start()
    return copies


def relative_evens(shard):
    count = lax.axis_size("dp")
    bits = count.bit_length() - 1
    evens = list(range(0, count, 2))
    if shard == 1:
        evens.sort(key=lambda k: [k >> b & 1 for b in range(1, bits)])
    return evens


def put_grad(grad, s, scratch, keep_ref, send_ref, me, rows):
    if rows % 16:
        keep_ref[...] = grad
        return
    scratch[...] = grad
    for n, k in enumerate(relative_evens(s)):
        for k_of, ref in ((k, keep_ref), (k ^ 1, send_ref)):
            start = pl.multiple_of(jnp.bitwise_xor(me, k_of) * rows, 16)
            ref[n] = scratch[pl.ds(start, rows), :].astype(ref.dtype)


def grad_shapes(width, rows, cols):
    if rows % 16:
        return [((width, cols), F32), ((8, 128), BF16)] * 2
    half = width // rows // 2
    return [((half, rows, cols), BF16)] * 4


def scatter_core(keep, send, s, rows):
    if rows % 16:
        me = lax.axis_index("dp")
        blocks = keep.reshape(-1, rows, keep.shape[-1])
        evens = jnp.array(relative_evens(s))
        keep = jnp.take(blocks, me ^ evens, axis=0)
        send = jnp.take(blocks, me ^ evens ^ 1, axis=0).astype(BF16)
    return keep.astype(F32) + swap(send, "dp", 1).astype(F32)


def scatter_split(now):
    half = now.shape[0] // 2
    return now[:half], now[half:].astype(BF16)


def scatter_step(kept, sent, s, n):
    return kept + swap(sent, "dp", bit_orders()[s][:-1][::-1][n]).astype(F32)


def scatter_end(own, other):
    return own + swap(other.astype(BF16), "tensor", 2).astype(F32)


def spread_columns(value, index, count):
    rows, cols = value.shape
    return lax.dynamic_update_slice(jnp.zeros((rows, count * cols), F32), value, (0, index * cols))


def plus_swapped(value, axis, bit):
    return value + swap(value, axis, bit)


def norm_first_body(x_ref, g_ref, xh_ref, dy_ref, sum_ref):
    xh_ref[...] = normalize(x_ref[...])[0].astype(BF16)
    grad = g_ref[...]
    dy_ref[...] = grad.astype(BF16)
    sum_ref[...] = column_sum(grad)


def causal_mask(length):
    rows = lax.broadcasted_iota(jnp.int32, (length, length), 0)
    cols = lax.broadcasted_iota(jnp.int32, (length, length), 1)
    return rows >= cols


def attend_body(plan, n_arrays, head_cols, *refs):
    ids, own, other, vec, biases = refs[:5]
    pieces = refs[5 : 5 + n_arrays]
    outs, (lse_out, a_out, keep, send, total, sems) = refs[5 + n_arrays : 11 + n_arrays], refs[11 + n_arrays :]
    w, qkv_out, ctx_out = outs[0:2], outs[2:4], outs[4:6]
    me, role = ids[0], ids[1]
    copies = place_pieces(pieces, plan, w, sems, me)
    rows = own.shape[0]
    gain, shift = vec[0:1, :], vec[1:2, :]
    for ref, at in ((own, role), (other, 1 - role)):
        a_rows = ref[...].astype(F32) * gain + shift
        a_out[pl.ds(pl.multiple_of(at * rows, rows), rows), :] = a_rows.astype(BF16)
    for copy in copies:
        copy.wait()
    seq = 2 * rows
    a_rows = a_out[...]
    mask = causal_mask(seq)
    lane = lax.broadcasted_iota(jnp.int32, (seq, 128), 1)
    lse_all = jnp.zeros((seq, 128), F32)
    heads = head_cols // HEAD_DIM
    attn = None
    for s in range(2):
        qkv = dot(a_rows, w[s][:, : 3 * head_cols]) + biases[s : s + 1, :]
        qkv = qkv.astype(BF16)
        qkv_out[s][...] = qkv
        parts = []
        for h in range(heads):
            q, k, v = (
                qkv[:, n * head_cols + h * HEAD_DIM : n * head_cols + (h + 1) * HEAD_DIM]
                for n in range(3)
            )
            scores = jnp.where(mask, dot(q, k, NT) * SCALE, MASK_LOW)
            top = jnp.max(scores, axis=-1, keepdims=True)
            lse = top + jnp.log(jnp.sum(jnp.exp(scores - top), axis=-1, keepdims=True))
            lse_all = jnp.where(lane == s * heads + h, lse, lse_all)
            probs = jnp.exp(scores - lse).astype(BF16)
            parts.append(dot(probs, v).astype(BF16))
        ctx = jnp.concatenate(parts, axis=1)
        ctx_out[s][...] = ctx
        add = dot(ctx, w[s][:, 3 * head_cols :], NT)
        attn = add if attn is None else attn + add
    lse_out[...] = lse_all
    total[...] = attn
    keep[...] = total[pl.ds(pl.multiple_of(role * rows, rows), rows), :]
    send[...] = total[pl.ds(pl.multiple_of((1 - role) * rows, rows), rows), :].astype(BF16)


def norm_second_body(x_ref, keep_ref, recv_ref, vec_ref, resid_ref, m_ref):
    resid = x_ref[...] + (keep_ref[...] + recv_ref[...].astype(F32)) + vec_ref[4:5, :]
    resid_ref[...] = resid
    normed, _ = normalize(resid)
    m_ref[...] = (normed * vec_ref[5:6, :] + vec_ref[6:7, :]).astype(BF16)


def feed_body(plan, n_arrays, hidden, *refs):
    ids, m_own, m_other, dy_own, dy_other, bias = refs[:6]
    pieces = refs[6 : 6 + n_arrays]
    act_out, dpre_out = refs[6 + n_arrays : 8 + n_arrays], refs[8 + n_arrays : 10 + n_arrays]
    m_out, dy_out, dm_keep, dm_send, br_keep, br_send, sum_out, w, sems = refs[10 + n_arrays :]
    copies = place_pieces(pieces, plan, (w.at[0], w.at[1]), sems, ids[0])
    rows = m_own.shape[0]
    m_out[:rows] = m_own[...]
    m_out[rows:] = m_other[...]
    dy_out[:rows] = dy_own[...]
    dy_out[rows:] = dy_other[...]
    m, dy = m_out[...], dy_out[...]
    for copy in copies:
        copy.wait()
    d_m = branch = None
    for s in range(2):
        w_fc, w_proj = w[s, :, :hidden], w[s, :, hidden:]
        pre = dot(m, w_fc) + bias[s : s + 1, :]
        act, slope = gelu_parts(pre)
        act_low = act.astype(BF16)
        act_out[s][...] = act_low
        d_pre = dot(dy, w_proj) * slope
        sum_out[s : s + 1, :] = column_sum(d_pre)
        d_pre_low = d_pre.astype(BF16)
        dpre_out[s][...] = d_pre_low
        one, two = dot(d_pre_low, w_fc, NT), dot(act_low, w_proj, NT)
        d_m = one if d_m is None else d_m + one
        branch = two if branch is None else branch + two
    dm_keep[...] = d_m[:rows]
    dm_send[...] = d_m[rows:].astype(BF16)
    br_keep[...] = branch[:rows]
    br_send[...] = branch[rows:].astype(BF16)


def feed_grad_body(block_rows, s, ids, m_ref, dy_ref, act_ref, dpre_ref, keep, send, scratch):
    grad = jnp.concatenate(
        [dot(m_ref[...], dpre_ref[...], TN), dot(dy_ref[...], act_ref[...], TN)], axis=1
    )
    put_grad(grad, s, scratch, keep, send, ids[0], block_rows)


def norm_second_back_body(resid_ref, keep_ref, recv_ref, grad_ref, vec_ref, grad1_ref, dz_ref, sum_ref):
    d_m = keep_ref[...] + recv_ref[...].astype(F32)
    normed, inv = normalize(resid_ref[...])
    grad1 = grad_ref[...] + norm_back(d_m, normed, inv, vec_ref[5:6, :])
    grad1_ref[...] = grad1
    dz_ref[...] = grad1.astype(BF16)
    sum_ref[0:1, :] = column_sum(grad1)
    sum_ref[1:2, :] = column_sum(d_m * normed)
    sum_ref[2:3, :] = column_sum(d_m)


def attend_back_body(block_rows, head_cols, s, *refs):
    ids, own, other, w, qkv_ref, lse_ref, a_ref, ctx_ref = refs[:8]
    last = s == 0
    if last:
        da_before, xh_own, xh_other = refs[8:11]
    keep_g, send_g, sum_heads = refs[11:14] if last else refs[8:11]
    outs = refs[14:] if last else refs[11:]
    dz, scratch = outs[-2:]
    role = ids[1]
    rows = own.shape[0]
    seq = 2 * rows
    mine = pl.ds(pl.multiple_of(role * rows, rows), rows)
    theirs = pl.ds(pl.multiple_of((1 - role) * rows, rows), rows)
    dz[mine, :] = own[...]
    dz[theirs, :] = other[...]
    mask = causal_mask(seq)
    heads = head_cols // HEAD_DIM
    d_ctx_all = dot(dz[...], w[:, 3 * head_cols :]).astype(BF16)
    d_parts = [[], [], []]
    qkv = qkv_ref[...]
    for h in range(heads):
        q, k, v = (
            qkv[:, n * head_cols + h * HEAD_DIM : n * head_cols + (h + 1) * HEAD_DIM]
            for n in range(3)
        )
        d_ctx = d_ctx_all[:, h * HEAD_DIM : (h + 1) * HEAD_DIM]
        head = s * heads + h
        scores = jnp.where(mask, dot(q, k, NT) * SCALE, MASK_LOW)
        probs = jnp.exp(scores - lse_ref[:, head : head + 1])
        d_parts[2].append(dot(probs.astype(BF16), d_ctx, TN))
        d_probs = dot(d_ctx, v, NT)
        row_sum = jnp.sum(probs * d_probs, axis=-1, keepdims=True)
        d_scores = (probs * (d_probs - row_sum) * SCALE).astype(BF16)
        d_parts[0].append(dot(d_scores, k))
        d_parts[1].append(dot(d_scores, q, TN))
    d_qkv = jnp.concatenate(d_parts[0] + d_parts[1] + d_parts[2], axis=1)
    sum_heads[...] = column_sum(d_qkv)
    d_qkv = d_qkv.astype(BF16)
    grad = jnp.concatenate([dot(a_ref[...], d_qkv, TN), dot(dz[...], ctx_ref[...], TN)], axis=1)
    put_grad(grad, s, scratch, keep_g, send_g, ids[0], block_rows)
    d_a = dot(d_qkv, w[:, : 3 * head_cols], NT)
    if not last:
        outs[0][...] = d_a
        return
    keep, send, sum_wide, total, normed = outs[:5]
    d_a = d_a + da_before[...]
    total[...] = d_a
    normed[mine, :] = xh_own[...]
    normed[theirs, :] = xh_other[...]
    sum_wide[0:1, :] = column_sum(d_a * normed[...].astype(F32))
    sum_wide[1:2, :] = column_sum(d_a)
    keep[...] = total[mine, :]
    send[...] = total[theirs, :].astype(BF16)


def sums_body(head_cols, ids, wide, heads_own, heads_other, second, fc_sum, bp_sum, vec_out):
    z = ids[2]
    vec_out[0:2, :] = wide[0:2, :]
    vec_out[4:7, :] = second[0:3, :]
    vec_out[7:8, :] = bp_sum[...]

    def placed(own, other, t):
        zero = jnp.zeros_like(own)
        return jnp.where(z == t, own, zero) + jnp.where(jnp.bitwise_xor(z, 2) == t, other, zero)

    n_z = vec_out.shape[1] // head_cols
    for row, part in ((2, 0), (3, 2)):
        own, other = (
            ref[:, part * head_cols : (part + 1) * head_cols] for ref in (heads_own, heads_other)
        )
        vec_out[row : row + 1, :] = jnp.concatenate(
            [placed(own, other, t) for t in range(n_z)], axis=1
        )
    for t in range(vec_out.shape[0] - 8):
        vec_out[8 + t : 9 + t, :] = placed(fc_sum[0:1, :], fc_sum[1:2, :], t)


def norm_first_back_body(x_ref, keep_ref, recv_ref, grad1_ref, vec_ref, out_ref):
    d_a = keep_ref[...] + recv_ref[...].astype(F32)
    normed, inv = normalize(x_ref[...])
    out_ref[...] = grad1_ref[...] + norm_back(d_a, normed, inv, vec_ref[0:1, :])


def shards(inputs, qkv_weight, out_weight, fc_weight, proj_weight, vectors, out_grad):
    rows, width = inputs.shape
    head_cols = qkv_weight.shape[3]
    hidden = fc_weight.shape[2]
    block_rows = qkv_weight.shape[1]
    vec_rows, vec_cols = vectors.shape[1:]
    n_z = lax.axis_size("tensor")
    n_dp = lax.axis_size("dp")
    z = lax.axis_index("tensor")
    me = lax.axis_index("dp")
    shard_ids = (z, z ^ 2)
    ids = jnp.stack([me, z & 1, z]).astype(jnp.int32)
    smem = {0: pltpu.SMEM}
    row = (rows, width)
    seq = 2 * rows
    both = (seq, width)

    part_a = jnp.concatenate(
        [qkv_weight[0].reshape(block_rows, 3 * head_cols), out_weight[0].T], axis=1
    )
    part_b = jnp.concatenate([fc_weight[0], proj_weight[0].T], axis=1)
    bits = bit_orders()[0]
    stages = len(bits)
    vec = spread_columns(vectors[0], me * n_z + z, n_dp * n_z)
    pieces_a = gather_start(part_a)
    vec = plus_swapped(vec, "tensor", 1)
    vec = plus_swapped(vec, "dp", bits[0])
    normed1, dy, bp_sum = call(
        norm_first_body, "norm_first", 2, [(row, BF16), (row, BF16), ((1, width), F32)], (inputs, out_grad)
    )
    pieces_a, vec, part_b, normed1, dy = tied(pieces_a, vec, part_b, normed1, dy)
    normed1_other = swap(normed1, "tensor", 1)
    pieces_b = gather_start(part_b)
    for stage in range(stages):
        pieces_a = gather_stage(pieces_a, stage)
        if stage < stages - 2:
            vec = plus_swapped(vec, "dp", bits[stage + 1])
            pieces_a, vec, normed1_other = tied(pieces_a, vec, normed1_other)
        elif stage == stages - 2:
            vec = plus_swapped(vec, "tensor", 3)
            flat, vec = tied(pieces_a + pieces_b, vec)
            pieces_a, pieces_b = flat[:2], flat[2:]
        else:
            vec = plus_swapped(vec, "dp", bits[stage])
    pieces_b = gather_stage(pieces_b, 0)
    arrays_a, plan_a = piece_plan(pieces_a)

    def of_shard(table):
        return jnp.stack([lax.dynamic_index_in_dim(table, s, 0, False) for s in shard_ids])

    bias_q = of_shard(vec[2].reshape(n_z, head_cols))
    bias_v = of_shard(vec[3].reshape(n_z, head_cols))
    biases = jnp.concatenate([bias_q, jnp.zeros_like(bias_q), bias_v], axis=1)
    bias_fc = of_shard(vec[8:].reshape(n_z, hidden))

    def any_space(first, arrays):
        return {**smem, **{first + n: pl.ANY for n in range(len(arrays))}}

    w_0, w_1, qkv_0, qkv_1, ctx_0, ctx_1, lse, a_seq, attn_keep, attn_send = call(
        lambda *refs: attend_body(plan_a, len(arrays_a), head_cols, *refs),
        "attend",
        6,
        [((width, 4 * head_cols), BF16)] * 2
        + [((seq, 3 * head_cols), BF16)] * 2
        + [((seq, head_cols), BF16)] * 2
        + [((seq, 128), F32), (both, BF16), (row, F32), (row, BF16)],
        (ids, normed1, normed1_other, vec, biases, *arrays_a),
        [pltpu.VMEM(both, F32), pltpu.SemaphoreType.DMA((len(plan_a),))],
        any_space(5, arrays_a),
    )
    pieces_b, attn_send = tied(pieces_b, attn_send)
    attn_recv = swap(attn_send, "tensor", 1)
    for stage in range(1, stages - 1):
        pieces_b = gather_stage(pieces_b, stage)
    resid1, m = call(
        norm_second_body,
        "norm_second",
        2,
        [(row, F32), (row, BF16)],
        (inputs, attn_keep, attn_recv, vec),
    )
    m_other = swap(m, "tensor", 1)
    dy_other = swap(dy, "tensor", 1)
    pieces_b, m_other, dy_other = tied(pieces_b, m_other, dy_other)
    pieces_b = gather_stage(pieces_b, stages - 1)
    arrays_b, plan_b = piece_plan(pieces_b)
    act_0, act_1, d_pre_0, d_pre_1, m_both, dy_both, dm_keep, dm_send, br_keep, br_send, fc_sum = call(
        lambda *refs: feed_body(plan_b, len(arrays_b), hidden, *refs),
        "feed",
        7,
        [((seq, hidden), BF16)] * 4
        + [(both, BF16), (both, BF16), (row, F32), (row, BF16), (row, F32), (row, BF16), ((2, hidden), F32)],
        (ids, m, m_other, dy, dy_other, bias_fc, *arrays_b),
        [pltpu.VMEM((2, width, 2 * hidden), BF16), pltpu.SemaphoreType.DMA((len(plan_b),))],
        any_space(6, arrays_b),
    )
    dm_recv = swap(dm_send, "tensor", 1)

    def feed_grad(s, act, d_pre):
        return call(
            lambda *refs: feed_grad_body(block_rows, s, *refs),
            "feed_grad_" + str(s),
            3,
            grad_shapes(width, block_rows, 2 * hidden)[:2],
            (ids, m_both, dy_both, act, d_pre),
            [pltpu.VMEM((width, 2 * hidden), F32)],
            smem,
        )

    parts_1 = feed_grad(1, act_1, d_pre_1)
    split_b1 = scatter_split(scatter_core(*parts_1, 1, block_rows))
    parts_0 = feed_grad(0, act_0, d_pre_0)
    dm_recv, *flat = together(dm_recv, *parts_0, *split_b1)
    parts_0, split_b1 = flat[:2], flat[2:]
    br_recv = swap(br_send, "tensor", 1)
    grad1, dz, second_sums = call(
        norm_second_back_body,
        "norm_second_back",
        2,
        [(row, F32), (row, BF16), ((3, width), F32)],
        (resid1, dm_keep, dm_recv, out_grad, vec),
    )
    split_b0 = scatter_split(scatter_core(*parts_0, 0, block_rows))
    dz, br_recv, *split_b0 = together(dz, br_recv, *split_b0)
    dz_other = swap(dz, "tensor", 1)
    split_b = [split_b0, split_b1]
    outputs = resid1 + (br_keep + br_recv.astype(F32)) + vec[7]

    def attend_back(s, w, qkv, ctx, more_args, more_outs, more_scratch):
        return call(
            lambda *refs: attend_back_body(block_rows, head_cols, s, *refs),
            "attend_back_" + str(s),
            6,
            grad_shapes(width, block_rows, 4 * head_cols)[:2] + [((1, 3 * head_cols), F32)] + more_outs,
            (ids, dz, dz_other, w, qkv, lse, a_seq, ctx, *more_args),
            more_scratch + [pltpu.VMEM(both, BF16), pltpu.VMEM((width, 4 * head_cols), F32)],
            smem,
        )

    halvings = stages - 1
    keep_1, send_1, head_sums_1, da_1 = attend_back(1, w_1, qkv_1, ctx_1, (), [(both, F32)], [])
    halvings = stages - 1
    now_b = [scatter_step(*split_b[s], s, 0) for s in range(2)]
    split_b = [scatter_split(now) for now in now_b]
    da_1, *flat = together(da_1, *split_b[0], *split_b[1])
    split_b = [flat[:2], flat[2:]]
    split_1 = scatter_split(scatter_core(keep_1, send_1, 1, block_rows))
    da_1, *split_1 = together(da_1, *split_1)
    keep_0, send_0, head_sums_0, da_keep, da_send, wide_sums = attend_back(
        0,
        w_0,
        qkv_0,
        ctx_0,
        (da_1, normed1, normed1_other),
        [(row, F32), (row, BF16), ((2, width), F32)],
        [pltpu.VMEM(both, F32), pltpu.VMEM(both, BF16)],
    )
    for n in range(1, halvings):
        now_b = [scatter_step(*split_b[s], s, n) for s in range(2)]
        if n < halvings - 1:
            split_b = [scatter_split(now) for now in now_b]
    now_1 = scatter_step(*split_1, 1, 0)
    split_1 = scatter_split(now_1)
    da_send, wide_sums, *flat = together(da_send, wide_sums, *split_1, *now_b)
    split_1, now_b = flat[:2], flat[2:]
    da_recv = swap(da_send, "tensor", 1)
    b_recv = swap(now_b[1][0].astype(BF16), "tensor", 2)
    split_0 = scatter_split(scatter_core(keep_0, send_0, 0, block_rows))
    (vec_sum,) = call(
        lambda *refs: sums_body(head_cols, *refs),
        "sums",
        1,
        [((vec_rows, width), F32)],
        (ids, wide_sums, head_sums_0, head_sums_1, second_sums, fc_sum, bp_sum),
        (),
        smem,
    )
    vec_sum = plus_swapped(vec_sum, "dp", 1)
    *split_0, vec_sum = together(*split_0, vec_sum)
    for n in range(halvings):
        now_0 = scatter_step(*split_0, 0, n)
        vec_sum = plus_swapped(vec_sum, "dp", bits[:-1][::-1][n])
        if n + 1 < halvings:
            now_1 = scatter_step(*split_1, 1, n + 1)
            split_0 = scatter_split(now_0)
            split_1 = scatter_split(now_1) if n + 2 < halvings else (now_1,)
            if n == 0:
                b_recv, da_recv, vec_sum = together(b_recv, da_recv, vec_sum)
            *flat, vec_sum = together(*split_0, *split_1, vec_sum)
            split_0, split_1 = flat[:2], flat[2:]
    b_grad = now_b[0][0] + b_recv.astype(F32)
    vec_sum = vec_sum + swap(vec_sum, "tensor", 1) + swap(vec_sum, "tensor", 2) + swap(vec_sum, "tensor", 3)
    a_grad = scatter_end(now_0[0], split_1[0][0])
    vector_grad = lax.dynamic_slice_in_dim(vec_sum, (me * n_z + z) * vec_cols, vec_cols, 1)
    (input_grad,) = call(
        norm_first_back_body,
        "norm_first_back",
        2,
        [(row, F32)],
        (inputs, da_keep, da_recv, grad1, vec),
    )
    qkv_grad = a_grad[:, : 3 * head_cols].reshape(block_rows, 3, head_cols)
    return (
        outputs,
        input_grad,
        qkv_grad[None],
        a_grad[:, 3 * head_cols :].T[None],
        b_grad[None, :, :hidden],
        b_grad[:, hidden:].T[None],
        vector_grad[None],
    )


def solution(mesh):
    rows = P(("dp", "tensor"), None)
    weights = (
        P(None, "dp", None, "tensor"),
        P(None, "tensor", "dp"),
        P(None, "dp", "tensor"),
        P(None, "tensor", "dp"),
        P(None, None, ("dp", "tensor")),
    )
    return jax.shard_map(
        shards,
        mesh=mesh,
        in_specs=(rows, *weights, rows),
        out_specs=(rows, rows, *weights),
        check_vma=False,
    )
```

```python
import jax
import jax.numpy as jnp
from jax import lax
from jax.experimental import pallas as pl
from jax.experimental.pallas import tpu as pltpu
from jax.sharding import PartitionSpec as P

HEAD_DIM = 64
NORM_EPS = 1e-05
GELU_COEF = 0.7978845608028654
MASK_LOW = -1000000000.0
SCALE = HEAD_DIM ** (-0.5)
BF16 = jnp.bfloat16
F32 = jnp.float32
NN = ((1,), (0,))
NT = ((1,), (1,))
TN = ((0,), (0,))


def dot(a, b, dims=NN):
    return lax.dot_general(a, b, (dims, ((), ())), preferred_element_type=F32)


def swap(value, axis, bits):
    size = lax.axis_size(axis)
    return lax.ppermute(value, axis, [(i, i ^ bits) for i in range(size)])


def normalize(rows):
    mean = jnp.mean(rows, axis=-1, keepdims=True)
    centred = rows - mean
    variance = jnp.mean(centred * centred, axis=-1, keepdims=True)
    inv_std = lax.rsqrt(variance + NORM_EPS)
    return (centred * inv_std, inv_std)


def norm_back(grad_out, normed, inv_std, gain):
    grad_normed = grad_out * gain
    mean_one = jnp.mean(grad_normed, axis=-1, keepdims=True)
    mean_two = jnp.mean(grad_normed * normed, axis=-1, keepdims=True)
    return inv_std * (grad_normed - mean_one - normed * mean_two)


def gelu_parts(pre):
    square = pre * pre
    inner = GELU_COEF * (pre + 0.044715 * square * pre)
    tanh_val = jnp.tanh(inner)
    half = 0.5 * (1.0 + tanh_val)
    value = pre * half
    slope = half + 0.5 * pre * (1.0 - tanh_val * tanh_val) * GELU_COEF * (
        1.0 + 3.0 * 0.044715 * square
    )
    return (value, slope)


def column_sum(value):
    return jnp.sum(value, axis=0, keepdims=True)


def together(*values):
    return lax.optimization_barrier(values)


def call(body, name, micros, outs, args, scratch=(), spaces=None):
    spaces = spaces or {}
    in_specs = [
        pl.BlockSpec(memory_space=spaces.get(n, pltpu.VMEM)) for n in range(len(args))
    ]
    return pl.pallas_call(
        body,
        name=name,
        out_shape=[jax.ShapeDtypeStruct(shape, dtype) for shape, dtype in outs],
        in_specs=in_specs,
        out_specs=[pl.BlockSpec(memory_space=pltpu.VMEM) for _ in outs],
        scratch_shapes=list(scratch),
        compiler_params=pltpu.CompilerParams(vmem_limit_bytes=56 * 1024 * 1024),
        cost_estimate=pl.CostEstimate(
            flops=int(micros * 5e7), bytes_accessed=int(micros * 1e5), transcendentals=0
        ),
    )(*args)


def bit_orders():
    count = lax.axis_size("dp").bit_length() - 1
    bits = [1 << b for b in range(1, count)]
    return (bits + [1], bits[::-1] + [1])


def gather_start(piece):
    return [[((0,), piece[None])], [((0,), swap(piece[None], "tensor", 2))]]


def with_columns(held, columns):
    (ks, value), = held
    return [(ks, jnp.concatenate([value, columns[None]], axis=2))]


def gather_stage(pieces, stage):
    out = []
    for held, order in zip(pieces, bit_orders()):
        bit = order[stage]
        while len(held) > 4:
            held = [
                (held[n][0] + held[n + 1][0], jnp.concatenate([held[n][1], held[n + 1][1]]))
                for n in range(0, len(held), 2)
            ]
        out.append(held + [(tuple(k ^ bit for k in ks), swap(v, "dp", bit)) for ks, v in held])
    return out


def tied(pieces, *values):
    flat, tree = jax.tree.flatten([[v for _, v in held] for held in pieces])
    done = together(*flat, *values)
    arrays = jax.tree.unflatten(tree, done[: len(flat)])
    pieces = [
        [(ks, v) for (ks, _), v in zip(held, new)] for held, new in zip(pieces, arrays)
    ]
    return (pieces, *done[len(flat) :])


def assembled(held):
    ks = [k for group, _ in held for k in group]
    stacked = jnp.concatenate([v for _, v in held])
    slot = [ks.index(k) for k in range(len(ks))]
    stacked = jnp.stack([stacked[n] for n in slot])
    whole = jnp.take(stacked, lax.axis_index("dp") ^ jnp.arange(len(ks)), axis=0)
    return whole.reshape(1, -1, whole.shape[-1])


def piece_plan(pieces):
    aligned = pieces[0][0][1].shape[1] % 16 == 0
    arrays, plan = [], []
    for s, held in enumerate(pieces):
        if not aligned:
            plan.append((len(arrays), 0, s, None))
            arrays.append(assembled(held))
            continue
        for ks, value in held:
            plan += [(len(arrays), slot, s, k) for slot, k in enumerate(ks)]
            arrays.append(value)
    return arrays, plan


def place_pieces(refs, plan, dst_refs, sems, me):
    copies = []
    for n, (array, slot, s, k) in enumerate(plan):
        rows = refs[array].shape[1]
        if k is None:
            target = dst_refs[s]
        else:
            start = pl.multiple_of(jnp.bitwise_xor(me, k) * rows, 16)
            target = dst_refs[s].at[pl.ds(start, rows), :]
        copies.append(pltpu.make_async_copy(refs[array].at[slot], target, sems.at[n]))
    for copy in copies:
        copy.start()
    return copies


def relative_evens(shard):
    count = lax.axis_size("dp")
    bits = count.bit_length() - 1
    evens = list(range(0, count, 2))
    if shard == 1:
        evens.sort(key=lambda k: [k >> b & 1 for b in range(1, bits)])
    return evens


def put_grad(grad, s, scratch, keep_ref, send_ref, me, rows):
    if rows % 16:
        keep_ref[...] = grad
        return
    scratch[...] = grad
    for n, k in enumerate(relative_evens(s)):
        for k_of, ref in ((k, keep_ref), (k ^ 1, send_ref)):
            start = pl.multiple_of(jnp.bitwise_xor(me, k_of) * rows, 16)
            ref[n] = scratch[pl.ds(start, rows), :].astype(ref.dtype)


def grad_shapes(width, rows, cols):
    if rows % 16:
        return [((width, cols), F32), ((8, 128), BF16)] * 2
    half = width // rows // 2
    return [((half, rows, cols), BF16)] * 4


def scatter_core(keep, send, s, rows):
    if rows % 16:
        me = lax.axis_index("dp")
        blocks = keep.reshape(-1, rows, keep.shape[-1])
        evens = jnp.array(relative_evens(s))
        keep = jnp.take(blocks, me ^ evens, axis=0)
        send = jnp.take(blocks, me ^ evens ^ 1, axis=0).astype(BF16)
    return keep.astype(F32) + swap(send, "dp", 1).astype(F32)


def scatter_split(now):
    half = now.shape[0] // 2
    return now[:half], now[half:].astype(BF16)


def scatter_send(sent, s, n):
    return swap(sent, "dp", bit_orders()[s][:-1][::-1][n]).astype(F32)


def scatter_step(kept, sent, s, n):
    return kept + scatter_send(sent, s, n)


def scatter_on(kept, sent, s, first, halvings):
    for n in range(first, halvings):
        now = scatter_step(kept, sent, s, n)
        if n < halvings - 1:
            kept, sent = scatter_split(now)
    return now[0]


def scatter_end(own, other):
    return own + swap(other.astype(BF16), "tensor", 2).astype(F32)


def from_tensor(value):
    return [value] + [swap(value, "tensor", k) for k in (1, 2, 3)]


def norm_first_body(x_ref, g_ref, xh_ref, dy_ref, sum_ref):
    xh_ref[...] = normalize(x_ref[...])[0].astype(BF16)
    grad = g_ref[...]
    dy_ref[...] = grad.astype(BF16)
    sum_ref[...] = column_sum(grad)


def table_body(ids, own, one, two, three, out, wide):
    cols, table = own.shape
    wide[...] = jnp.zeros_like(wide)
    for k, ref in enumerate((own, one, two, three)):
        for r in range(4):
            @pl.when(jnp.bitwise_xor(ids[2], k) == r)
            def _(ref=ref, r=r):
                wide[r * cols : (r + 1) * cols, 0:table] = ref[...]
    rest = wide[...]
    terms = []
    for _ in range(3):
        term = rest.astype(BF16)
        rest = rest - term.astype(F32)
        terms.append(term)
    out[...] = jnp.concatenate([t[:, :16] for t in terms] + [jnp.zeros_like(terms[0][:, :80])], axis=1)


def causal_mask(length):
    rows = lax.broadcasted_iota(jnp.int32, (length, length), 0)
    cols = lax.broadcasted_iota(jnp.int32, (length, length), 1)
    return rows >= cols


def attend_body(plan, n_arrays, head_cols, *refs):
    ids, own, other = refs[:3]
    pieces = refs[3 : 3 + n_arrays]
    outs, (lse_out, a_out, keep, send, vec, total, sems) = refs[3 + n_arrays : 9 + n_arrays], refs[9 + n_arrays :]
    w, qkv_out, ctx_out = outs[0:2], outs[2:4], outs[4:6]
    me, role = ids[0], ids[1]
    copies = place_pieces(pieces, plan, w, sems, me)
    rows = own.shape[0]
    for copy in copies:
        copy.wait()
    terms = w[0][:, 4 * head_cols :].astype(F32).T
    vec[...] = terms[0:16] + terms[16:32] + terms[32:48]
    gain, shift = vec[0:1, :], vec[1:2, :]
    for ref, at in ((own, role), (other, 1 - role)):
        a_rows = ref[...].astype(F32) * gain + shift
        a_out[pl.ds(pl.multiple_of(at * rows, rows), rows), :] = a_rows.astype(BF16)

    def of_shard(row, s):
        shard = jnp.bitwise_xor(ids[2], 2 * s)
        value = jnp.zeros((1, head_cols), F32)
        for t in range(vec.shape[1] // head_cols):
            part = vec[row : row + 1, t * head_cols : (t + 1) * head_cols]
            value = jnp.where(shard == t, part, value)
        return value

    seq = 2 * rows
    a_rows = a_out[...]
    mask = causal_mask(seq)
    lane = lax.broadcasted_iota(jnp.int32, (seq, 128), 1)
    lse_all = jnp.zeros((seq, 128), F32)
    heads = head_cols // HEAD_DIM
    attn = None
    for s in range(2):
        bias = [of_shard(2, s), jnp.zeros((1, head_cols), F32), of_shard(3, s)]
        qkv = dot(a_rows, w[s][:, : 3 * head_cols]) + jnp.concatenate(bias, axis=1)
        qkv = qkv.astype(BF16)
        qkv_out[s][...] = qkv
        parts = []
        for h in range(heads):
            q, k, v = (
                qkv[:, n * head_cols + h * HEAD_DIM : n * head_cols + (h + 1) * HEAD_DIM]
                for n in range(3)
            )
            scores = jnp.where(mask, dot(q, k, NT) * SCALE, MASK_LOW)
            top = jnp.max(scores, axis=-1, keepdims=True)
            lse = top + jnp.log(jnp.sum(jnp.exp(scores - top), axis=-1, keepdims=True))
            lse_all = jnp.where(lane == s * heads + h, lse, lse_all)
            probs = jnp.exp(scores - lse).astype(BF16)
            parts.append(dot(probs, v).astype(BF16))
        ctx = jnp.concatenate(parts, axis=1)
        ctx_out[s][...] = ctx
        add = dot(ctx, w[s][:, 3 * head_cols : 4 * head_cols], NT)
        attn = add if attn is None else attn + add
    lse_out[...] = lse_all
    total[...] = attn
    keep[...] = total[pl.ds(pl.multiple_of(role * rows, rows), rows), :]
    send[...] = total[pl.ds(pl.multiple_of((1 - role) * rows, rows), rows), :].astype(BF16)


def norm_second_body(x_ref, keep_ref, recv_ref, vec_ref, resid_ref, m_ref):
    resid = x_ref[...] + (keep_ref[...] + recv_ref[...].astype(F32)) + vec_ref[4:5, :]
    resid_ref[...] = resid
    normed, _ = normalize(resid)
    m_ref[...] = (normed * vec_ref[5:6, :] + vec_ref[6:7, :]).astype(BF16)


def feed_body(plan, n_arrays, hidden, *refs):
    ids, m_own, m_other, dy_own, dy_other, vec = refs[:6]
    pieces = refs[6 : 6 + n_arrays]
    act_out, dpre_out = refs[6 + n_arrays : 8 + n_arrays], refs[8 + n_arrays : 10 + n_arrays]
    m_out, dy_out, dm_keep, dm_send, br_keep, br_send, sum_out, w, sems = refs[10 + n_arrays :]
    copies = place_pieces(pieces, plan, (w.at[0], w.at[1]), sems, ids[0])
    rows = m_own.shape[0]
    m_out[:rows] = m_own[...]
    m_out[rows:] = m_other[...]
    dy_out[:rows] = dy_own[...]
    dy_out[rows:] = dy_other[...]
    m, dy = m_out[...], dy_out[...]
    d_m = branch = None
    for s in range(2):
        for entry, copy in zip(plan, copies):
            if entry[2] == s:
                copy.wait()
        w_fc, w_proj = w[s, :, :hidden], w[s, :, hidden:]
        bias = vec[pl.ds(8 + jnp.bitwise_xor(ids[2], 2 * s), 1), :]
        pre = dot(m, w_fc) + bias
        act, slope = gelu_parts(pre)
        act_low = act.astype(BF16)
        act_out[s][...] = act_low
        d_pre = dot(dy, w_proj) * slope
        sum_out[s : s + 1, :] = column_sum(d_pre)
        d_pre_low = d_pre.astype(BF16)
        dpre_out[s][...] = d_pre_low
        one, two = dot(d_pre_low, w_fc, NT), dot(act_low, w_proj, NT)
        d_m = one if d_m is None else d_m + one
        branch = two if branch is None else branch + two
    dm_keep[...] = d_m[:rows]
    dm_send[...] = d_m[rows:].astype(BF16)
    br_keep[...] = branch[:rows]
    br_send[...] = branch[rows:].astype(BF16)


def feed_grad_body(block_rows, s, ids, m_ref, dy_ref, act_ref, dpre_ref, keep, send, scratch):
    grad = jnp.concatenate(
        [dot(m_ref[...], dpre_ref[...], TN), dot(dy_ref[...], act_ref[...], TN)], axis=1
    )
    put_grad(grad, s, scratch, keep, send, ids[0], block_rows)


def norm_second_back_body(resid_ref, keep_ref, recv_ref, grad_ref, vec_ref, grad1_ref, dz_ref, sum_ref):
    d_m = keep_ref[...] + recv_ref[...].astype(F32)
    normed, inv = normalize(resid_ref[...])
    grad1 = grad_ref[...] + norm_back(d_m, normed, inv, vec_ref[5:6, :])
    grad1_ref[...] = grad1
    dz_ref[...] = grad1.astype(BF16)
    sum_ref[0:1, :] = column_sum(grad1)
    sum_ref[1:2, :] = column_sum(d_m * normed)
    sum_ref[2:3, :] = column_sum(d_m)


def attend_back_body(block_rows, head_cols, s, *refs):
    ids, own, other, w, qkv_ref, lse_ref, a_ref, ctx_ref = refs[:8]
    last = s == 0
    if last:
        da_before, xh_own, xh_other, heads_other, second, fc_sum, bp_sum = refs[8:15]
        keep_g, send_g, keep, send, total, normed, table, dz, scratch = refs[15:]
    else:
        keep_g, send_g, heads_out, da_out, dz, scratch = refs[8:]
    role = ids[1]
    rows = own.shape[0]
    seq = 2 * rows
    mine = pl.ds(pl.multiple_of(role * rows, rows), rows)
    theirs = pl.ds(pl.multiple_of((1 - role) * rows, rows), rows)
    dz[mine, :] = own[...]
    dz[theirs, :] = other[...]
    mask = causal_mask(seq)
    heads = head_cols // HEAD_DIM
    d_ctx_all = dot(dz[...], w[:, 3 * head_cols : 4 * head_cols]).astype(BF16)
    d_parts = [[], [], []]
    qkv = qkv_ref[...]
    for h in range(heads):
        q, k, v = (
            qkv[:, n * head_cols + h * HEAD_DIM : n * head_cols + (h + 1) * HEAD_DIM]
            for n in range(3)
        )
        d_ctx = d_ctx_all[:, h * HEAD_DIM : (h + 1) * HEAD_DIM]
        head = s * heads + h
        scores = jnp.where(mask, dot(q, k, NT) * SCALE, MASK_LOW)
        probs = jnp.exp(scores - lse_ref[:, head : head + 1])
        d_parts[2].append(dot(probs.astype(BF16), d_ctx, TN))
        d_probs = dot(d_ctx, v, NT)
        row_sum = jnp.sum(probs * d_probs, axis=-1, keepdims=True)
        d_scores = (probs * (d_probs - row_sum) * SCALE).astype(BF16)
        d_parts[0].append(dot(d_scores, k))
        d_parts[1].append(dot(d_scores, q, TN))
    d_qkv = jnp.concatenate(d_parts[0] + d_parts[1] + d_parts[2], axis=1)
    heads_own = column_sum(d_qkv)
    d_qkv = d_qkv.astype(BF16)
    grads = [dot(a_ref[...], d_qkv, TN), dot(dz[...], ctx_ref[...], TN)]
    d_a = dot(d_qkv, w[:, : 3 * head_cols], NT)
    if not last:
        heads_out[...] = heads_own
        da_out[...] = d_a
        put_grad(jnp.concatenate(grads, axis=1), s, scratch, keep_g, send_g, ids[0], block_rows)
        return
    d_a = d_a + da_before[...]
    total[...] = d_a
    keep[...] = total[mine, :]
    send[...] = total[theirs, :].astype(BF16)
    normed[mine, :] = xh_own[...]
    normed[theirs, :] = xh_other[...]
    z = ids[2]

    def placed(own_value, other_value, t):
        zero = jnp.zeros_like(own_value)
        return jnp.where(z == t, own_value, zero) + jnp.where(
            jnp.bitwise_xor(z, 2) == t, other_value, zero
        )

    table[...] = jnp.zeros_like(table)
    table[0:1, :] = column_sum(d_a * normed[...].astype(F32))
    table[1:2, :] = column_sum(d_a)
    n_z = table.shape[1] // head_cols
    for row, part in ((2, 0), (3, 2)):
        cols = slice(part * head_cols, (part + 1) * head_cols)
        table[row : row + 1, :] = jnp.concatenate(
            [placed(heads_own[:, cols], heads_other[:, cols], t) for t in range(n_z)], axis=1
        )
    table[4:7, :] = second[0:3, :]
    table[7:8, :] = bp_sum[...]
    for t in range(n_z):
        table[8 + t : 9 + t, :] = placed(fc_sum[0:1, :], fc_sum[1:2, :], t)
    grads.append(table[...].T)
    put_grad(jnp.concatenate(grads, axis=1), s, scratch, keep_g, send_g, ids[0], block_rows)


def norm_first_back_body(x_ref, keep_ref, recv_ref, grad1_ref, vec_ref, out_ref):
    d_a = keep_ref[...] + recv_ref[...].astype(F32)
    normed, inv = normalize(x_ref[...])
    out_ref[...] = grad1_ref[...] + norm_back(d_a, normed, inv, vec_ref[0:1, :])


def shards(inputs, qkv_weight, out_weight, fc_weight, proj_weight, vectors, out_grad):
    rows, width = inputs.shape
    head_cols = qkv_weight.shape[3]
    hidden = fc_weight.shape[2]
    block_rows = qkv_weight.shape[1]
    vec_rows, vec_cols = vectors.shape[1:]
    n_z = lax.axis_size("tensor")
    n_dp = lax.axis_size("dp")
    z = lax.axis_index("tensor")
    me = lax.axis_index("dp")
    shard_ids = (z, z ^ 2)
    ids = jnp.stack([me, z & 1, z]).astype(jnp.int32)
    smem = {0: pltpu.SMEM}
    row = (rows, width)
    seq = 2 * rows
    both = (seq, width)

    part_a = jnp.concatenate(
        [qkv_weight[0].reshape(block_rows, 3 * head_cols), out_weight[0].T], axis=1
    )
    part_b = jnp.concatenate([fc_weight[0], proj_weight[0].T], axis=1)
    bits = bit_orders()[0]
    stages = len(bits)
    parts_v = from_tensor(vectors[0].T)
    pieces_a = gather_start(part_a)
    normed1, dy, bp_sum = call(
        norm_first_body, "norm_first", 2, [(row, BF16), (row, BF16), ((1, width), F32)], (inputs, out_grad)
    )
    (table,) = call(
        table_body,
        "table",
        1,
        [((n_z * vec_cols, 128), BF16)],
        (ids, *parts_v),
        [pltpu.VMEM((n_z * vec_cols, 128), F32)],
        smem,
    )
    pieces_a, part_b, normed1, table = tied(pieces_a, part_b, normed1, table)
    pieces_a[0] = with_columns(pieces_a[0], table)
    normed1_other = swap(normed1, "tensor", 1)
    pieces_b = gather_start(part_b)
    for stage in range(stages):
        pieces_a = gather_stage(pieces_a, stage)
        if stage < stages - 2:
            pieces_a, normed1_other = tied(pieces_a, normed1_other)
        elif stage == stages - 2:
            (flat,) = tied(pieces_a + pieces_b)
            pieces_a, pieces_b = flat[:2], flat[2:]
    pieces_b = gather_stage(pieces_b, 0)
    arrays_a, plan_a = piece_plan(pieces_a)

    def any_space(first, arrays):
        return {**smem, **{first + n: pl.ANY for n in range(len(arrays))}}

    w_0, w_1, qkv_0, qkv_1, ctx_0, ctx_1, lse, a_seq, attn_keep, attn_send, vec = call(
        lambda *refs: attend_body(plan_a, len(arrays_a), head_cols, *refs),
        "attend",
        6,
        [((width, 4 * head_cols + 128), BF16), ((width, 4 * head_cols), BF16)]
        + [((seq, 3 * head_cols), BF16)] * 2
        + [((seq, head_cols), BF16)] * 2
        + [((seq, 128), F32), (both, BF16), (row, F32), (row, BF16), ((16, width), F32)],
        (ids, normed1, normed1_other, *arrays_a),
        [pltpu.VMEM(both, F32), pltpu.SemaphoreType.DMA((len(plan_a),))],
        any_space(3, arrays_a),
    )
    pieces_b, attn_send = tied(pieces_b, attn_send)
    attn_recv = swap(attn_send, "tensor", 1)
    for stage in range(1, stages - 1):
        pieces_b = gather_stage(pieces_b, stage)
    resid1, m = call(
        norm_second_body,
        "norm_second",
        2,
        [(row, F32), (row, BF16)],
        (inputs, attn_keep, attn_recv, vec),
    )
    m_other = swap(m, "tensor", 1)
    dy_other = swap(dy, "tensor", 1)
    pieces_b, m_other, dy_other = tied(pieces_b, m_other, dy_other)
    pieces_b = gather_stage(pieces_b, stages - 1)
    arrays_b, plan_b = piece_plan(pieces_b)
    act_0, act_1, d_pre_0, d_pre_1, m_both, dy_both, dm_keep, dm_send, br_keep, br_send, fc_sum = call(
        lambda *refs: feed_body(plan_b, len(arrays_b), hidden, *refs),
        "feed",
        7,
        [((seq, hidden), BF16)] * 4
        + [(both, BF16), (both, BF16), (row, F32), (row, BF16), (row, F32), (row, BF16), ((2, hidden), F32)],
        (ids, m, m_other, dy, dy_other, vec, *arrays_b),
        [pltpu.VMEM((2, width, 2 * hidden), BF16), pltpu.SemaphoreType.DMA((len(plan_b),))],
        any_space(6, arrays_b),
    )
    dm_recv = swap(dm_send, "tensor", 1)

    def feed_grad(s, act, d_pre):
        return call(
            lambda *refs: feed_grad_body(block_rows, s, *refs),
            "feed_grad_" + str(s),
            3,
            grad_shapes(width, block_rows, 2 * hidden)[:2],
            (ids, m_both, dy_both, act, d_pre),
            [pltpu.VMEM((width, 2 * hidden), F32)],
            smem,
        )

    parts_1 = feed_grad(1, act_1, d_pre_1)
    split_b1 = scatter_split(scatter_core(*parts_1, 1, block_rows))
    parts_0 = feed_grad(0, act_0, d_pre_0)
    dm_recv, *flat = together(dm_recv, *parts_0, *split_b1)
    parts_0, split_b1 = flat[:2], flat[2:]
    br_recv = swap(br_send, "tensor", 1)
    grad1, dz, second_sums = call(
        norm_second_back_body,
        "norm_second_back",
        2,
        [(row, F32), (row, BF16), ((3, width), F32)],
        (resid1, dm_keep, dm_recv, out_grad, vec),
    )
    split_b0 = scatter_split(scatter_core(*parts_0, 0, block_rows))
    dz, br_recv, *split_b0 = together(dz, br_recv, *split_b0)
    dz_other = swap(dz, "tensor", 1)
    split_b = [split_b0, split_b1]
    outputs = resid1 + (br_keep + br_recv.astype(F32)) + vec[7]

    def attend_back(s, w, qkv, ctx, more_args, more_outs, more_scratch):
        cols = 4 * head_cols + 128 * (1 - s)
        return call(
            lambda *refs: attend_back_body(block_rows, head_cols, s, *refs),
            "attend_back_" + str(s),
            6,
            grad_shapes(width, block_rows, cols)[:2] + more_outs,
            (ids, dz, dz_other, w, qkv, lse, a_seq, ctx, *more_args),
            more_scratch + [pltpu.VMEM(both, BF16), pltpu.VMEM((width, cols), F32)],
            smem,
        )

    halvings = stages - 1
    keep_1, send_1, head_sums_1, da_1 = attend_back(
        1, w_1, qkv_1, ctx_1, (), [((1, 3 * head_cols), F32), (both, F32)], []
    )
    halvings = stages - 1
    split_b = [scatter_split(scatter_step(*split_b[s], s, 0)) for s in range(2)]
    da_1, *flat = together(da_1, *split_b[0], *split_b[1])
    split_b = [flat[:2], flat[2:]]
    split_1 = scatter_split(scatter_core(keep_1, send_1, 1, block_rows))
    da_1, *split_1 = together(da_1, *split_1)
    keep_0, send_0, da_keep, da_send = attend_back(
        0,
        w_0,
        qkv_0,
        ctx_0,
        (da_1, normed1, normed1_other, head_sums_1, second_sums, fc_sum, bp_sum),
        [(row, F32), (row, BF16)],
        [pltpu.VMEM(both, F32), pltpu.VMEM(both, BF16), pltpu.VMEM((128, width), F32)],
    )
    b_own, b_other = split_b
    b_other = scatter_on(*b_other, 1, 1, halvings)
    now_1 = scatter_step(*split_1, 1, 0)
    split_1 = scatter_split(now_1)
    split_0 = scatter_split(scatter_core(keep_0, send_0, 0, block_rows))
    da_send, b_other, *flat = together(da_send, b_other, *split_1, *b_own)
    split_1, b_own = flat[:2], flat[2:]
    da_recv = swap(da_send, "tensor", 1)
    b_recv = swap(b_other.astype(BF16), "tensor", 2)
    b_own = scatter_on(*b_own, 0, 1, halvings)
    for n in range(halvings):
        now_0 = scatter_step(*split_0, 0, n)
        if n + 1 < halvings:
            now_1 = scatter_step(*split_1, 1, n + 1)
            split_0 = scatter_split(now_0)
            split_1 = scatter_split(now_1) if n + 2 < halvings else (now_1,)
            b_recv, b_own, da_recv, *flat = together(b_recv, b_own, da_recv, *split_0, *split_1)
            split_0, split_1 = flat[:2], flat[2:]
    b_grad = b_own + b_recv.astype(F32)
    table_sum = now_0[0][:, 4 * head_cols :]
    table_sum = sum(from_tensor(table_sum[:, :16]))
    a_grad = scatter_end(now_0[0][:, : 4 * head_cols], split_1[0][0])
    vector_grad = lax.dynamic_slice_in_dim(table_sum[:, :vec_rows], z * vec_cols, vec_cols, 0).T
    (input_grad,) = call(
        norm_first_back_body,
        "norm_first_back",
        2,
        [(row, F32)],
        (inputs, da_keep, da_recv, grad1, vec),
    )
    qkv_grad = a_grad[:, : 3 * head_cols].reshape(block_rows, 3, head_cols)
    return (
        outputs,
        input_grad,
        qkv_grad[None],
        a_grad[:, 3 * head_cols :].T[None],
        b_grad[None, :, :hidden],
        b_grad[:, hidden:].T[None],
        vector_grad[None],
    )


def solution(mesh):
    rows = P(("dp", "tensor"), None)
    weights = (
        P(None, "dp", None, "tensor"),
        P(None, "tensor", "dp"),
        P(None, "dp", "tensor"),
        P(None, "tensor", "dp"),
        P(None, None, ("dp", "tensor")),
    )
    return jax.shard_map(
        shards,
        mesh=mesh,
        in_specs=(rows, *weights, rows),
        out_specs=(rows, rows, *weights),
        check_vma=False,
    )
```

```python
import jax
import jax.numpy as jnp
from jax import lax
from jax.experimental import pallas as pl
from jax.experimental.pallas import tpu as pltpu
from jax.sharding import PartitionSpec as P

HEAD_DIM = 64
NORM_EPS = 1e-05
GELU_COEF = 0.7978845608028654
MASK_LOW = -1000000000.0
SCALE = HEAD_DIM ** (-0.5)
BF16 = jnp.bfloat16
F32 = jnp.float32
NN = ((1,), (0,))
NT = ((1,), (1,))
TN = ((0,), (0,))


def dot(a, b, dims=NN):
    return lax.dot_general(a, b, (dims, ((), ())), preferred_element_type=F32)


def swap(value, axis, bits):
    size = lax.axis_size(axis)
    return lax.ppermute(value, axis, [(i, i ^ bits) for i in range(size)])


def normalize(rows):
    mean = jnp.mean(rows, axis=-1, keepdims=True)
    centred = rows - mean
    variance = jnp.mean(centred * centred, axis=-1, keepdims=True)
    inv_std = lax.rsqrt(variance + NORM_EPS)
    return (centred * inv_std, inv_std)


def norm_back(grad_out, normed, inv_std, gain):
    grad_normed = grad_out * gain
    mean_one = jnp.mean(grad_normed, axis=-1, keepdims=True)
    mean_two = jnp.mean(grad_normed * normed, axis=-1, keepdims=True)
    return inv_std * (grad_normed - mean_one - normed * mean_two)


def gelu_parts(pre):
    square = pre * pre
    inner = GELU_COEF * (pre + 0.044715 * square * pre)
    tanh_val = jnp.tanh(inner)
    half = 0.5 * (1.0 + tanh_val)
    value = pre * half
    slope = half + 0.5 * pre * (1.0 - tanh_val * tanh_val) * GELU_COEF * (
        1.0 + 3.0 * 0.044715 * square
    )
    return (value, slope)


def column_sum(value):
    return jnp.sum(value, axis=0, keepdims=True)


def together(*values):
    return lax.optimization_barrier(values)


def call(body, name, micros, outs, args, scratch=(), spaces=None):
    spaces = spaces or {}
    in_specs = [
        pl.BlockSpec(memory_space=spaces.get(n, pltpu.VMEM)) for n in range(len(args))
    ]
    return pl.pallas_call(
        body,
        name=name,
        out_shape=[jax.ShapeDtypeStruct(shape, dtype) for shape, dtype in outs],
        in_specs=in_specs,
        out_specs=[pl.BlockSpec(memory_space=pltpu.VMEM) for _ in outs],
        scratch_shapes=list(scratch),
        compiler_params=pltpu.CompilerParams(vmem_limit_bytes=56 * 1024 * 1024),
        cost_estimate=pl.CostEstimate(
            flops=int(micros * 5e7), bytes_accessed=int(micros * 1e5), transcendentals=0
        ),
    )(*args)


def bit_orders():
    count = lax.axis_size("dp").bit_length() - 1
    bits = [1 << b for b in range(1, count)]
    return (bits + [1], bits[::-1] + [1])


def gather_start(piece):
    return [[((0,), piece[None])], [((0,), swap(piece[None], "tensor", 2))]]


def with_columns(held, columns):
    (ks, value), = held
    return [(ks, jnp.concatenate([value, columns[None]], axis=2))]


def gather_stage(pieces, stage):
    out = []
    for held, order in zip(pieces, bit_orders()):
        bit = order[stage]
        while len(held) > 4:
            held = [
                (held[n][0] + held[n + 1][0], jnp.concatenate([held[n][1], held[n + 1][1]]))
                for n in range(0, len(held), 2)
            ]
        out.append(held + [(tuple(k ^ bit for k in ks), swap(v, "dp", bit)) for ks, v in held])
    return out


def tied(pieces, *values):
    flat, tree = jax.tree.flatten([[v for _, v in held] for held in pieces])
    done = together(*flat, *values)
    arrays = jax.tree.unflatten(tree, done[: len(flat)])
    pieces = [
        [(ks, v) for (ks, _), v in zip(held, new)] for held, new in zip(pieces, arrays)
    ]
    return (pieces, *done[len(flat) :])


def assembled(held):
    ks = [k for group, _ in held for k in group]
    stacked = jnp.concatenate([v for _, v in held])
    slot = [ks.index(k) for k in range(len(ks))]
    stacked = jnp.stack([stacked[n] for n in slot])
    whole = jnp.take(stacked, lax.axis_index("dp") ^ jnp.arange(len(ks)), axis=0)
    return whole.reshape(1, -1, whole.shape[-1])


def piece_plan(pieces):
    aligned = pieces[0][0][1].shape[1] % 16 == 0
    arrays, plan = [], []
    for s, held in enumerate(pieces):
        if not aligned:
            plan.append((len(arrays), 0, s, None))
            arrays.append(assembled(held))
            continue
        for ks, value in held:
            plan += [(len(arrays), slot, s, k) for slot, k in enumerate(ks)]
            arrays.append(value)
    return arrays, plan


def place_pieces(refs, plan, dst_refs, sems, me):
    copies = []
    for n, (array, slot, s, k) in enumerate(plan):
        rows = refs[array].shape[1]
        if k is None:
            target = dst_refs[s]
        else:
            start = pl.multiple_of(jnp.bitwise_xor(me, k) * rows, 16)
            target = dst_refs[s].at[pl.ds(start, rows), :]
        copies.append(pltpu.make_async_copy(refs[array].at[slot], target, sems.at[n]))
    for copy in copies:
        copy.start()
    return copies


def relative_evens(shard):
    count = lax.axis_size("dp")
    bits = count.bit_length() - 1
    evens = list(range(0, count, 2))
    if shard == 1:
        evens.sort(key=lambda k: [k >> b & 1 for b in range(1, bits)])
    return evens


def put_grad(grad, s, scratch, low_ref, high_ref, send_ref, me, rows):
    if rows % 16:
        low_ref[...] = grad
        return
    scratch[...] = grad
    half = low_ref.shape[0]
    for n, k in enumerate(relative_evens(s)):
        keep_ref, at = (low_ref, n) if n < half else (high_ref, n - half)
        for k_of, ref, slot in ((k, keep_ref, at), (k ^ 1, send_ref, n)):
            start = pl.multiple_of(jnp.bitwise_xor(me, k_of) * rows, 16)
            ref[slot] = scratch[pl.ds(start, rows), :].astype(ref.dtype)


def grad_shapes(width, rows, cols):
    if rows % 16:
        return [((width, cols), F32), ((8, 128), BF16), ((8, 128), BF16)]
    half = width // rows // 2
    return [((half // 2, rows, cols), BF16)] * 2 + [((half, rows, cols), BF16)]


def scatter_core(low, high, send, s, rows):
    if rows % 16:
        me = lax.axis_index("dp")
        blocks = low.reshape(-1, rows, low.shape[-1])
        evens = jnp.array(relative_evens(s))
        send = jnp.take(blocks, me ^ evens ^ 1, axis=0).astype(BF16)
        keep = jnp.take(blocks, me ^ evens, axis=0)
        low, high = keep[: len(evens) // 2], keep[len(evens) // 2 :]
    half = low.shape[0]
    came = swap(send, "dp", 1)
    stays = low.astype(F32) + came[:half].astype(F32)
    return stays, (high.astype(F32) + came[half:].astype(F32)).astype(BF16)


def scatter_split(now):
    half = now.shape[0] // 2
    return now[:half], now[half:].astype(BF16)


def scatter_send(sent, s, n):
    return swap(sent, "dp", bit_orders()[s][:-1][::-1][n]).astype(F32)


def scatter_step(kept, sent, s, n):
    return kept + scatter_send(sent, s, n)


def scatter_on(kept, sent, s, first, halvings):
    for n in range(first, halvings):
        now = scatter_step(kept, sent, s, n)
        if n < halvings - 1:
            kept, sent = scatter_split(now)
    return now[0]


def scatter_end(own, other):
    return own + swap(other.astype(BF16), "tensor", 2).astype(F32)


def from_tensor(value):
    return [value] + [swap(value, "tensor", k) for k in (1, 2, 3)]


def norm_first_body(x_ref, g_ref, xh_ref, dy_ref, sum_ref):
    xh_ref[...] = normalize(x_ref[...])[0].astype(BF16)
    grad = g_ref[...]
    dy_ref[...] = grad.astype(BF16)
    sum_ref[...] = column_sum(grad)


def table_body(ids, own, one, two, three, out, wide):
    cols, table = own.shape
    wide[...] = jnp.zeros_like(wide)
    for k, ref in enumerate((own, one, two, three)):
        for r in range(4):
            @pl.when(jnp.bitwise_xor(ids[2], k) == r)
            def _(ref=ref, r=r):
                wide[r * cols : (r + 1) * cols, 0:table] = ref[...]
    rest = wide[...]
    terms = []
    for _ in range(3):
        term = rest.astype(BF16)
        rest = rest - term.astype(F32)
        terms.append(term)
    out[...] = jnp.concatenate([t[:, :16] for t in terms] + [jnp.zeros_like(terms[0][:, :80])], axis=1)


def causal_mask(length):
    rows = lax.broadcasted_iota(jnp.int32, (length, length), 0)
    cols = lax.broadcasted_iota(jnp.int32, (length, length), 1)
    return rows >= cols


def attend_body(plan, n_arrays, head_cols, *refs):
    ids, own, other = refs[:3]
    pieces = refs[3 : 3 + n_arrays]
    outs, (lse_out, a_out, keep, send, vec, total, sems) = refs[3 + n_arrays : 9 + n_arrays], refs[9 + n_arrays :]
    w, qkv_out, ctx_out = outs[0:2], outs[2:4], outs[4:6]
    me, role = ids[0], ids[1]
    copies = place_pieces(pieces, plan, w, sems, me)
    rows = own.shape[0]
    for copy in copies:
        copy.wait()
    terms = w[0][:, 4 * head_cols :].astype(F32).T
    vec[...] = terms[0:16] + terms[16:32] + terms[32:48]
    gain, shift = vec[0:1, :], vec[1:2, :]
    for ref, at in ((own, role), (other, 1 - role)):
        a_rows = ref[...].astype(F32) * gain + shift
        a_out[pl.ds(pl.multiple_of(at * rows, rows), rows), :] = a_rows.astype(BF16)

    def of_shard(row, s):
        shard = jnp.bitwise_xor(ids[2], 2 * s)
        value = jnp.zeros((1, head_cols), F32)
        for t in range(vec.shape[1] // head_cols):
            part = vec[row : row + 1, t * head_cols : (t + 1) * head_cols]
            value = jnp.where(shard == t, part, value)
        return value

    seq = 2 * rows
    a_rows = a_out[...]
    mask = causal_mask(seq)
    lane = lax.broadcasted_iota(jnp.int32, (seq, 128), 1)
    lse_all = jnp.zeros((seq, 128), F32)
    heads = head_cols // HEAD_DIM
    attn = None
    for s in range(2):
        bias = [of_shard(2, s), jnp.zeros((1, head_cols), F32), of_shard(3, s)]
        qkv = dot(a_rows, w[s][:, : 3 * head_cols]) + jnp.concatenate(bias, axis=1)
        qkv = qkv.astype(BF16)
        qkv_out[s][...] = qkv
        parts = []
        for h in range(heads):
            q, k, v = (
                qkv[:, n * head_cols + h * HEAD_DIM : n * head_cols + (h + 1) * HEAD_DIM]
                for n in range(3)
            )
            scores = jnp.where(mask, dot(q, k, NT) * SCALE, MASK_LOW)
            top = jnp.max(scores, axis=-1, keepdims=True)
            lse = top + jnp.log(jnp.sum(jnp.exp(scores - top), axis=-1, keepdims=True))
            lse_all = jnp.where(lane == s * heads + h, lse, lse_all)
            probs = jnp.exp(scores - lse).astype(BF16)
            parts.append(dot(probs, v).astype(BF16))
        ctx = jnp.concatenate(parts, axis=1)
        ctx_out[s][...] = ctx
        add = dot(ctx, w[s][:, 3 * head_cols : 4 * head_cols], NT)
        attn = add if attn is None else attn + add
    lse_out[...] = lse_all
    total[...] = attn
    keep[...] = total[pl.ds(pl.multiple_of(role * rows, rows), rows), :]
    send[...] = total[pl.ds(pl.multiple_of((1 - role) * rows, rows), rows), :].astype(BF16)


def norm_second_body(x_ref, keep_ref, recv_ref, vec_ref, resid_ref, m_ref):
    resid = x_ref[...] + (keep_ref[...] + recv_ref[...].astype(F32)) + vec_ref[4:5, :]
    resid_ref[...] = resid
    normed, _ = normalize(resid)
    m_ref[...] = (normed * vec_ref[5:6, :] + vec_ref[6:7, :]).astype(BF16)


def feed_body(plan, n_arrays, hidden, block_rows, *refs):
    ids, m_own, m_other, dy_own, dy_other, vec = refs[:6]
    pieces = refs[6 : 6 + n_arrays]
    outs = refs[6 + n_arrays :]
    low_g, high_g, send_g, act_out, dpre_out = outs[:5]
    m_out, dy_out, dm_keep, dm_send, br_keep, br_send, sum_out, w, scratch, sems = outs[5:]
    copies = place_pieces(pieces, plan, (w.at[0], w.at[1]), sems, ids[0])
    rows = m_own.shape[0]
    m_out[:rows] = m_own[...]
    m_out[rows:] = m_other[...]
    dy_out[:rows] = dy_own[...]
    dy_out[rows:] = dy_other[...]
    m, dy = m_out[...], dy_out[...]
    d_m = branch = None
    for s in range(2):
        for entry, copy in zip(plan, copies):
            if entry[2] == s:
                copy.wait()
        w_fc, w_proj = w[s, :, :hidden], w[s, :, hidden:]
        bias = vec[pl.ds(8 + jnp.bitwise_xor(ids[2], 2 * s), 1), :]
        pre = dot(m, w_fc) + bias
        act, slope = gelu_parts(pre)
        act_low = act.astype(BF16)
        if s == 0:
            act_out[...] = act_low
        d_pre = dot(dy, w_proj) * slope
        sum_out[s : s + 1, :] = column_sum(d_pre)
        d_pre_low = d_pre.astype(BF16)
        if s == 0:
            dpre_out[...] = d_pre_low
        one, two = dot(d_pre_low, w_fc, NT), dot(act_low, w_proj, NT)
        d_m = one if d_m is None else d_m + one
        branch = two if branch is None else branch + two
    dm_keep[...] = d_m[:rows]
    dm_send[...] = d_m[rows:].astype(BF16)
    br_keep[...] = branch[:rows]
    br_send[...] = branch[rows:].astype(BF16)
    grad = jnp.concatenate([dot(m, d_pre_low, TN), dot(dy, act_low, TN)], axis=1)
    put_grad(grad, 1, scratch, low_g, high_g, send_g, ids[0], block_rows)


def feed_grad_body(block_rows, s, ids, m_ref, dy_ref, act_ref, dpre_ref, low, high, send, scratch):
    grad = jnp.concatenate(
        [dot(m_ref[...], dpre_ref[...], TN), dot(dy_ref[...], act_ref[...], TN)], axis=1
    )
    put_grad(grad, s, scratch, low, high, send, ids[0], block_rows)


def norm_second_back_body(resid_ref, keep_ref, recv_ref, grad_ref, vec_ref, grad1_ref, dz_ref, sum_ref):
    d_m = keep_ref[...] + recv_ref[...].astype(F32)
    normed, inv = normalize(resid_ref[...])
    grad1 = grad_ref[...] + norm_back(d_m, normed, inv, vec_ref[5:6, :])
    grad1_ref[...] = grad1
    dz_ref[...] = grad1.astype(BF16)
    sum_ref[0:1, :] = column_sum(grad1)
    sum_ref[1:2, :] = column_sum(d_m * normed)
    sum_ref[2:3, :] = column_sum(d_m)


def attend_back_body(block_rows, head_cols, s, *refs):
    ids, own, other, w, qkv_ref, lse_ref, a_ref, ctx_ref = refs[:8]
    last = s == 0
    if last:
        da_before, xh_own, xh_other, heads_other, second, fc_sum, bp_sum = refs[8:15]
        low_g, high_g, send_g, keep, send, total, normed, table, dz, scratch = refs[15:]
    else:
        low_g, high_g, send_g, heads_out, da_out, dz, scratch = refs[8:]
    role = ids[1]
    rows = own.shape[0]
    seq = 2 * rows
    mine = pl.ds(pl.multiple_of(role * rows, rows), rows)
    theirs = pl.ds(pl.multiple_of((1 - role) * rows, rows), rows)
    dz[mine, :] = own[...]
    dz[theirs, :] = other[...]
    mask = causal_mask(seq)
    heads = head_cols // HEAD_DIM
    d_ctx_all = dot(dz[...], w[:, 3 * head_cols : 4 * head_cols]).astype(BF16)
    d_parts = [[], [], []]
    qkv = qkv_ref[...]
    for h in range(heads):
        q, k, v = (
            qkv[:, n * head_cols + h * HEAD_DIM : n * head_cols + (h + 1) * HEAD_DIM]
            for n in range(3)
        )
        d_ctx = d_ctx_all[:, h * HEAD_DIM : (h + 1) * HEAD_DIM]
        head = s * heads + h
        scores = jnp.where(mask, dot(q, k, NT) * SCALE, MASK_LOW)
        probs = jnp.exp(scores - lse_ref[:, head : head + 1])
        d_parts[2].append(dot(probs.astype(BF16), d_ctx, TN))
        d_probs = dot(d_ctx, v, NT)
        row_sum = jnp.sum(probs * d_probs, axis=-1, keepdims=True)
        d_scores = (probs * (d_probs - row_sum) * SCALE).astype(BF16)
        d_parts[0].append(dot(d_scores, k))
        d_parts[1].append(dot(d_scores, q, TN))
    d_qkv = jnp.concatenate(d_parts[0] + d_parts[1] + d_parts[2], axis=1)
    heads_own = column_sum(d_qkv)
    d_qkv = d_qkv.astype(BF16)
    grads = [dot(a_ref[...], d_qkv, TN), dot(dz[...], ctx_ref[...], TN)]
    d_a = dot(d_qkv, w[:, : 3 * head_cols], NT)
    if not last:
        heads_out[...] = heads_own
        da_out[...] = d_a
        put_grad(jnp.concatenate(grads, axis=1), s, scratch, low_g, high_g, send_g, ids[0], block_rows)
        return
    d_a = d_a + da_before[...]
    total[...] = d_a
    keep[...] = total[mine, :]
    send[...] = total[theirs, :].astype(BF16)
    normed[mine, :] = xh_own[...]
    normed[theirs, :] = xh_other[...]
    z = ids[2]

    def placed(own_value, other_value, t):
        zero = jnp.zeros_like(own_value)
        return jnp.where(z == t, own_value, zero) + jnp.where(
            jnp.bitwise_xor(z, 2) == t, other_value, zero
        )

    table[...] = jnp.zeros_like(table)
    table[0:1, :] = column_sum(d_a * normed[...].astype(F32))
    table[1:2, :] = column_sum(d_a)
    n_z = table.shape[1] // head_cols
    for row, part in ((2, 0), (3, 2)):
        cols = slice(part * head_cols, (part + 1) * head_cols)
        table[row : row + 1, :] = jnp.concatenate(
            [placed(heads_own[:, cols], heads_other[:, cols], t) for t in range(n_z)], axis=1
        )
    table[4:7, :] = second[0:3, :]
    table[7:8, :] = bp_sum[...]
    for t in range(n_z):
        table[8 + t : 9 + t, :] = placed(fc_sum[0:1, :], fc_sum[1:2, :], t)
    grads.append(table[...].T)
    put_grad(jnp.concatenate(grads, axis=1), s, scratch, low_g, high_g, send_g, ids[0], block_rows)


def norm_first_back_body(x_ref, keep_ref, recv_ref, grad1_ref, vec_ref, out_ref):
    d_a = keep_ref[...] + recv_ref[...].astype(F32)
    normed, inv = normalize(x_ref[...])
    out_ref[...] = grad1_ref[...] + norm_back(d_a, normed, inv, vec_ref[0:1, :])


def shards(inputs, qkv_weight, out_weight, fc_weight, proj_weight, vectors, out_grad):
    rows, width = inputs.shape
    head_cols = qkv_weight.shape[3]
    hidden = fc_weight.shape[2]
    block_rows = qkv_weight.shape[1]
    vec_rows, vec_cols = vectors.shape[1:]
    n_z = lax.axis_size("tensor")
    n_dp = lax.axis_size("dp")
    z = lax.axis_index("tensor")
    me = lax.axis_index("dp")
    shard_ids = (z, z ^ 2)
    ids = jnp.stack([me, z & 1, z]).astype(jnp.int32)
    smem = {0: pltpu.SMEM}
    row = (rows, width)
    seq = 2 * rows
    both = (seq, width)

    part_a = jnp.concatenate(
        [qkv_weight[0].reshape(block_rows, 3 * head_cols), out_weight[0].T], axis=1
    )
    part_b = jnp.concatenate([fc_weight[0], proj_weight[0].T], axis=1)
    bits = bit_orders()[0]
    stages = len(bits)
    parts_v = from_tensor(vectors[0].T)
    pieces_a = gather_start(part_a)
    normed1, dy, bp_sum = call(
        norm_first_body, "norm_first", 2, [(row, BF16), (row, BF16), ((1, width), F32)], (inputs, out_grad)
    )
    (table,) = call(
        table_body,
        "table",
        1,
        [((n_z * vec_cols, 128), BF16)],
        (ids, *parts_v),
        [pltpu.VMEM((n_z * vec_cols, 128), F32)],
        smem,
    )
    pieces_a, part_b, normed1, table = tied(pieces_a, part_b, normed1, table)
    pieces_a[0] = with_columns(pieces_a[0], table)
    normed1_other = swap(normed1, "tensor", 1)
    pieces_b = gather_start(part_b)
    for stage in range(stages):
        pieces_a = gather_stage(pieces_a, stage)
        if stage < stages - 2:
            pieces_a, normed1_other = tied(pieces_a, normed1_other)
        elif stage == stages - 2:
            (flat,) = tied(pieces_a + pieces_b)
            pieces_a, pieces_b = flat[:2], flat[2:]
    pieces_b = gather_stage(pieces_b, 0)
    arrays_a, plan_a = piece_plan(pieces_a)

    def any_space(first, arrays):
        return {**smem, **{first + n: pl.ANY for n in range(len(arrays))}}

    w_0, w_1, qkv_0, qkv_1, ctx_0, ctx_1, lse, a_seq, attn_keep, attn_send, vec = call(
        lambda *refs: attend_body(plan_a, len(arrays_a), head_cols, *refs),
        "attend",
        6,
        [((width, 4 * head_cols + 128), BF16), ((width, 4 * head_cols), BF16)]
        + [((seq, 3 * head_cols), BF16)] * 2
        + [((seq, head_cols), BF16)] * 2
        + [((seq, 128), F32), (both, BF16), (row, F32), (row, BF16), ((16, width), F32)],
        (ids, normed1, normed1_other, *arrays_a),
        [pltpu.VMEM(both, F32), pltpu.SemaphoreType.DMA((len(plan_a),))],
        any_space(3, arrays_a),
    )
    pieces_b, attn_send = tied(pieces_b, attn_send)
    attn_recv = swap(attn_send, "tensor", 1)
    for stage in range(1, stages - 1):
        pieces_b = gather_stage(pieces_b, stage)
    resid1, m = call(
        norm_second_body,
        "norm_second",
        2,
        [(row, F32), (row, BF16)],
        (inputs, attn_keep, attn_recv, vec),
    )
    m_other = swap(m, "tensor", 1)
    dy_other = swap(dy, "tensor", 1)
    pieces_b, m_other, dy_other = tied(pieces_b, m_other, dy_other)
    pieces_b = gather_stage(pieces_b, stages - 1)
    arrays_b, plan_b = piece_plan(pieces_b)
    *parts_1, act_0, d_pre_0, m_both, dy_both, dm_keep, dm_send, br_keep, br_send, fc_sum = call(
        lambda *refs: feed_body(plan_b, len(arrays_b), hidden, block_rows, *refs),
        "feed",
        7,
        grad_shapes(width, block_rows, 2 * hidden)
        + [((seq, hidden), BF16)] * 2
        + [(both, BF16), (both, BF16), (row, F32), (row, BF16), (row, F32), (row, BF16), ((2, hidden), F32)],
        (ids, m, m_other, dy, dy_other, vec, *arrays_b),
        [
            pltpu.VMEM((2, width, 2 * hidden), BF16),
            pltpu.VMEM((width, 2 * hidden), F32),
            pltpu.SemaphoreType.DMA((len(plan_b),)),
        ],
        any_space(6, arrays_b),
    )
    dm_recv = swap(dm_send, "tensor", 1)

    split_b1 = scatter_core(*parts_1, 1, block_rows)
    parts_0 = call(
        lambda *refs: feed_grad_body(block_rows, 0, *refs),
        "feed_grad",
        3,
        grad_shapes(width, block_rows, 2 * hidden),
        (ids, m_both, dy_both, act_0, d_pre_0),
        [pltpu.VMEM((width, 2 * hidden), F32)],
        smem,
    )
    *parts_0, stays, goes = together(*parts_0, *split_b1)
    split_b1 = [stays, goes]
    br_recv = swap(br_send, "tensor", 1)
    dm_recv, *parts_0 = together(dm_recv, *parts_0)
    split_b0 = scatter_core(*parts_0, 0, block_rows)
    br_recv = swap(br_send, "tensor", 1)
    grad1, dz, second_sums = call(
        norm_second_back_body,
        "norm_second_back",
        2,
        [(row, F32), (row, BF16), ((3, width), F32)],
        (resid1, dm_keep, dm_recv, out_grad, vec),
    )
    dz, *split_b0 = together(dz, *split_b0)
    dz_other = swap(dz, "tensor", 1)
    split_b = [split_b0, split_b1]
    def attend_back(s, w, qkv, ctx, more_args, more_outs, more_scratch):
        cols = 4 * head_cols + 128 * (1 - s)
        return call(
            lambda *refs: attend_back_body(block_rows, head_cols, s, *refs),
            "attend_back_" + str(s),
            6,
            grad_shapes(width, block_rows, cols) + more_outs,
            (ids, dz, dz_other, w, qkv, lse, a_seq, ctx, *more_args),
            more_scratch + [pltpu.VMEM(both, BF16), pltpu.VMEM((width, cols), F32)],
            smem,
        )

    halvings = stages - 1
    *parts_1, head_sums_1, da_1 = attend_back(
        1, w_1, qkv_1, ctx_1, (), [((1, 3 * head_cols), F32), (both, F32)], []
    )
    halvings = stages - 1
    split_b = [scatter_split(scatter_step(*split_b[s], s, 0)) for s in range(2)]
    da_1, br_recv, *flat = together(da_1, br_recv, *split_b[0], *split_b[1])
    outputs = resid1 + (br_keep + br_recv.astype(F32)) + vec[7]
    split_b = [flat[:2], flat[2:]]
    split_1 = scatter_core(*parts_1, 1, block_rows)
    da_1, *split_1 = together(da_1, *split_1)
    *parts_0, da_keep, da_send = attend_back(
        0,
        w_0,
        qkv_0,
        ctx_0,
        (da_1, normed1, normed1_other, head_sums_1, second_sums, fc_sum, bp_sum),
        [(row, F32), (row, BF16)],
        [pltpu.VMEM(both, F32), pltpu.VMEM(both, BF16), pltpu.VMEM((128, width), F32)],
    )
    b_own, b_other = split_b
    b_other = scatter_on(*b_other, 1, 1, halvings)
    now_1 = scatter_step(*split_1, 1, 0)
    split_1 = scatter_split(now_1)
    split_0 = scatter_core(*parts_0, 0, block_rows)
    da_send, b_other, *flat = together(da_send, b_other, *split_1, *b_own)
    split_1, b_own = flat[:2], flat[2:]
    da_recv = swap(da_send, "tensor", 1)
    b_recv = swap(b_other.astype(BF16), "tensor", 2)
    b_own = scatter_on(*b_own, 0, 1, halvings)
    for n in range(halvings):
        now_0 = scatter_step(*split_0, 0, n)
        if n + 1 < halvings:
            now_1 = scatter_step(*split_1, 1, n + 1)
            split_0 = scatter_split(now_0)
            split_1 = scatter_split(now_1) if n + 2 < halvings else (now_1,)
            b_recv, b_own, da_recv, *flat = together(b_recv, b_own, da_recv, *split_0, *split_1)
            split_0, split_1 = flat[:2], flat[2:]
    b_grad = b_own + b_recv.astype(F32)
    table_sum = now_0[0][:, 4 * head_cols :]
    table_sum = sum(from_tensor(table_sum[:, :16]))
    a_grad = scatter_end(now_0[0][:, : 4 * head_cols], split_1[0][0])
    vector_grad = lax.dynamic_slice_in_dim(table_sum[:, :vec_rows], z * vec_cols, vec_cols, 0).T
    (input_grad,) = call(
        norm_first_back_body,
        "norm_first_back",
        2,
        [(row, F32)],
        (inputs, da_keep, da_recv, grad1, vec),
    )
    qkv_grad = a_grad[:, : 3 * head_cols].reshape(block_rows, 3, head_cols)
    return (
        outputs,
        input_grad,
        qkv_grad[None],
        a_grad[:, 3 * head_cols :].T[None],
        b_grad[None, :, :hidden],
        b_grad[:, hidden:].T[None],
        vector_grad[None],
    )


def solution(mesh):
    rows = P(("dp", "tensor"), None)
    weights = (
        P(None, "dp", None, "tensor"),
        P(None, "tensor", "dp"),
        P(None, "dp", "tensor"),
        P(None, "tensor", "dp"),
        P(None, None, ("dp", "tensor")),
    )
    return jax.shard_map(
        shards,
        mesh=mesh,
        in_specs=(rows, *weights, rows),
        out_specs=(rows, rows, *weights),
        check_vma=False,
    )
```
